32 devices in a mesh: net: 8 (over z, x), tm: 4 (over y, core).
Axes of the slice: x: 2, y: 2, z: 4, core: 2. Of those that a mesh axis runs over, the one named last changes fastest.
Arguments:
- initial: float32 [3, 128, 1024], P(None, 'net'), may hold values from -6 to 6
- wall_drag_factor: float32 [128], P('net'), may hold values from 0.05 to 0.5
- ground_exchange_rate: float32 [128], P('net'), may hold values from 0.02 to 0.3
- send_ends: int32 [8, 8, 8], P('net'), may hold values from -1 to 31, as said below
- recv_junction: int32 [8, 8, 8], P('net'), may hold values from -1 to 7, as said below
- slab_steps: int32 [4], P('tm'), may hold values from 4 to 8, as said below
Outputs:
- slab_ends: float32 [4, 3, 128, 1024], P('tm', None, 'net')
The draws below stay inside these ranges and needn't reach their ends.
Inputs may be any that keep to these rules, and one draw needn't show every extreme that they name: `send_ends`: entry [k, d, s] is an end of partition k whose junction partition d owns, or -1; the live entries of each list come first, every end of a partition appears exactly once in its lists, and in every draw each partition has one list to some owner that fills all 8 slots; each owner receives exactly 32 ends in all. `recv_junction`: entry [d, k, s] is live exactly where send_ends[k, d, s] is, and then names the owner-local junction of that end; every junction of every owner has at least one end. `slab_steps`: some slab takes 4 fine steps and some 2 * 4.
All inputs are finite; a program needn't handle non-finite values.
Results may differ from the reference program's by a relative error of at most 0.0001.
Values sent between devices are 32-bit elements; how exact they have to be, the bound alone decides.
A program may use at most 64 MiB of HBM per device.

```python
import math
import jax
import jax.numpy as jnp
from jax import lax

GROUP_CONDUITS = 16
CELLS = 1024
FINE_MIN = 4
ITERS = 1
STEPS_MAX = 8
JUNC_DEV = 8
NPIPE = 128
SLABS = 4
N_NET = 8


def network_lists(key):
    parts = N_NET
    ends_dev = 2 * GROUP_CONDUITS
    average = ends_dev // parts
    slot_count = 2 * average
    junctions = GROUP_CONDUITS // 2
    offset_order = jax.random.permutation(jax.random.fold_in(key, 101), parts)
    widths = jax.random.randint(jax.random.fold_in(key, 102), (parts // 2,), 0, average + 1)
    widths = widths.at[0].set(average)
    deltas = jnp.zeros((parts,), jnp.int32).at[offset_order[0::2]].set(widths).at[offset_order[1::2]].set(-widths)
    source_part = jnp.arange(parts, dtype=jnp.int32)[:, None]
    target_part = jnp.arange(parts, dtype=jnp.int32)[None, :]
    counts = average + deltas[(target_part - source_part) % parts]
    starts = jnp.cumsum(counts, axis=1) - counts
    end_keys = jax.random.split(jax.random.fold_in(key, 103), parts)
    end_order = jax.vmap(lambda one_key: jax.random.permutation(one_key, ends_dev))(end_keys)
    slot_ids = jnp.arange(slot_count, dtype=jnp.int32)
    active_mask = slot_ids[None, None, :] < counts[:, :, None]
    positions = jnp.clip(starts[:, :, None] + slot_ids[None, None, :], 0, ends_dev - 1)
    picked = end_order[jnp.arange(parts)[:, None, None], positions]
    send_table = jnp.where(active_mask, picked, -1).astype(jnp.int32)
    live_recv = jnp.transpose(active_mask, (1, 0, 2))
    score_keys = jax.random.split(jax.random.fold_in(key, 104), parts)
    scores = jax.vmap(lambda one_key: jax.random.permutation(one_key, parts * slot_count))(score_keys).reshape(parts, parts, slot_count)
    scores = jnp.where(live_recv, scores, scores + parts * slot_count)
    flat_scores = scores.reshape(parts, -1)
    ranks = jnp.argsort(jnp.argsort(flat_scores, axis=1, stable=True), axis=1, stable=True).reshape(parts, parts, slot_count)
    extra = jax.random.randint(jax.random.fold_in(key, 105), (parts, parts, slot_count), 0, junctions)
    chosen = jnp.where(ranks < junctions, ranks, extra)
    recv_table = jnp.where(live_recv, chosen, -1).astype(jnp.int32)
    return (send_table, recv_table)


def draw_send_ends(key, part):
    send_table, recv_table = network_lists(key)
    return send_table


def draw_recv_junction(key, part):
    send_table, recv_table = network_lists(key)
    return recv_table


def draw_slab_steps(key, part):
    values = jax.random.randint(jax.random.fold_in(key, 201), (SLABS,), FINE_MIN, 2 * FINE_MIN + 1)
    order = jax.random.permutation(jax.random.fold_in(key, 202), SLABS)
    values = values.at[order[0]].set(2 * FINE_MIN).at[order[1]].set(FINE_MIN)
    return values.astype(jnp.int32)


def levels(key, shape, cuts, least, high):
    gain = 1.0
    for axis_at, blocks in cuts:
        draws = jax.random.uniform(jax.random.fold_in(jax.random.fold_in(key, 6), axis_at), (blocks,), jnp.float32, least / len(cuts), high / len(cuts))
        gain = gain * jnp.repeat(jnp.exp(draws), shape[axis_at] // blocks).reshape((-1,) + (1,) * (len(shape) - 1 - axis_at))
    return gain


def centred(own_key, dims, spread, bound, cuts=(), kind=jnp.bfloat16):
    loudness = levels(own_key, dims, cuts, -0.22, 0.18) if cuts else 1.0
    result = jax.random.normal(own_key, dims, jnp.float32) * spread * loudness
    return jnp.minimum(jnp.maximum(result, -bound), bound).astype(kind)


def setup_inputs(seed: int = 0) -> dict:
    keys = jax.random.split(jax.random.key(seed), 7)
    initial = centred(keys[0], (3, NPIPE, CELLS), 1.0, 6.0, ((1, 8),), jnp.float32)
    wall_drag_factor = jnp.clip(jnp.exp(math.log(0.5) - 2.3025851 * jax.random.uniform(keys[1], (NPIPE,), jnp.float32) ** levels(keys[1], (NPIPE,), ((0, 8),), -0.2, 0.2)), 0.05, 0.5)
    ground_exchange_rate = jnp.clip(jnp.exp(math.log(0.3) - 2.7080503 * jax.random.uniform(keys[2], (NPIPE,), jnp.float32) ** levels(keys[2], (NPIPE,), ((0, 8),), -0.2, 0.2)), 0.02, 0.3)
    send_ends = draw_send_ends(jax.random.fold_in(keys[6], 71), 0)
    recv_junction = draw_recv_junction(jax.random.fold_in(keys[6], 71), 0)
    slab_steps = draw_slab_steps(jax.random.fold_in(keys[6], 71), 0)
    return {"initial": initial, "wall_drag_factor": wall_drag_factor, "ground_exchange_rate": ground_exchange_rate, "send_ends": send_ends, "recv_junction": recv_junction, "slab_steps": slab_steps}


def advect_quantity(state_buffers, entering_upstream, entering_downstream, upstream_warmth, downstream_warmth, clock_delta, wall_drag_factor, ground_exchange_rate):
    pressure = state_buffers[0]
    mass_flux = state_buffers[1]
    volume_heat_level = state_buffers[2]
    right_wave = pressure + mass_flux
    left_wave = pressure - mass_flux
    right_prev = jnp.concatenate([entering_upstream[:, None], right_wave[:, :-1]], 1)
    left_next = jnp.concatenate([left_wave[:, 1:], entering_downstream[:, None]], 1)
    right_new = right_wave - clock_delta * (right_wave - right_prev)
    left_new = left_wave - clock_delta * (left_wave - left_next)
    flux_star = 0.5 * (right_new - left_new)
    press_new = 0.5 * (right_new + left_new)
    flux_new = flux_star / (1.0 + clock_delta * wall_drag_factor[:, None] * jnp.abs(flux_star))
    stream_velocity = mass_flux / (1.0 + jnp.abs(mass_flux))
    prior_warmth = jnp.concatenate([upstream_warmth[:, None], volume_heat_level[:, :-1]], 1)
    coming_warmth = jnp.concatenate([volume_heat_level[:, 1:], downstream_warmth[:, None]], 1)
    carried_entries = volume_heat_level - clock_delta * (jnp.maximum(stream_velocity, 0.0) * (volume_heat_level - prior_warmth) + jnp.minimum(stream_velocity, 0.0) * (coming_warmth - volume_heat_level))
    temp_new = carried_entries / (1.0 + clock_delta * ground_exchange_rate[:, None])
    return jnp.stack([press_new, flux_new, temp_new], 0)


def junction_tables(send_ends, recv_junction):
    ends_dev = 2 * GROUP_CONDUITS
    owners = jnp.transpose(recv_junction, (1, 0, 2))
    source_part = jnp.arange(N_NET, dtype=jnp.int32)[:, None, None]
    target_part = jnp.arange(N_NET, dtype=jnp.int32)[None, :, None]
    valid = send_ends >= 0
    sender_boundary = jnp.where(valid, source_part * ends_dev + send_ends, 0).reshape(-1).astype(jnp.int32)
    junction_id = jnp.where(valid, target_part * JUNC_DEV + owners, N_NET * JUNC_DEV).reshape(-1).astype(jnp.int32)
    return valid.reshape(-1).astype(jnp.float32), sender_boundary, junction_id


def boundary_phantoms(state_buffers, lookup_matrices):
    active_mask, sender_boundary, junction_id = lookup_matrices
    pressure = state_buffers[0]
    mass_flux = state_buffers[1]
    volume_heat_level = state_buffers[2]
    left_out = (pressure[:, 0] - mass_flux[:, 0]).reshape(N_NET, GROUP_CONDUITS)
    right_out = (pressure[:, -1] + mass_flux[:, -1]).reshape(N_NET, GROUP_CONDUITS)
    departing_signal = jnp.concatenate([left_out, right_out], 1).reshape(-1)
    exit_warmth = jnp.concatenate([volume_heat_level[:, 0].reshape(N_NET, GROUP_CONDUITS), volume_heat_level[:, -1].reshape(N_NET, GROUP_CONDUITS)], 1).reshape(-1)
    slot_wave = departing_signal[sender_boundary] * active_mask
    position_warmth = exit_warmth[sender_boundary] * active_mask
    total = N_NET * JUNC_DEV + 1
    degree = jax.ops.segment_sum(active_mask, junction_id, total)[:-1]
    wave_mean = jax.ops.segment_sum(slot_wave, junction_id, total)[:-1] / degree
    temp_mean = jax.ops.segment_sum(position_warmth, junction_id, total)[:-1] / degree
    zero_one = jnp.zeros((1,), jnp.float32)
    wave_mean = jnp.concatenate([wave_mean, zero_one])
    temp_mean = jnp.concatenate([temp_mean, zero_one])
    ghost_wave = (2.0 * wave_mean[junction_id] - slot_wave) * active_mask
    ghost_temp = temp_mean[junction_id] * active_mask
    all_ends = N_NET * 2 * GROUP_CONDUITS
    wave_end = jax.ops.segment_sum(ghost_wave, sender_boundary, all_ends).reshape(N_NET, 2 * GROUP_CONDUITS)
    temp_end = jax.ops.segment_sum(ghost_temp, sender_boundary, all_ends).reshape(N_NET, 2 * GROUP_CONDUITS)
    return (wave_end[:, :GROUP_CONDUITS].reshape(-1), wave_end[:, GROUP_CONDUITS:].reshape(-1),
            temp_end[:, :GROUP_CONDUITS].reshape(-1), temp_end[:, GROUP_CONDUITS:].reshape(-1))


def reference(initial, wall_drag_factor, ground_exchange_rate, send_ends, recv_junction, slab_steps):
    lookup_matrices = junction_tables(send_ends, recv_junction)

    def advance(state_buffers, clock_delta):
        entering_upstream, entering_downstream, upstream_warmth, downstream_warmth = boundary_phantoms(state_buffers, lookup_matrices)
        return advect_quantity(state_buffers, entering_upstream, entering_downstream, upstream_warmth, downstream_warmth, clock_delta, wall_drag_factor, ground_exchange_rate)

    def coarse(state_buffers):
        return advance(state_buffers, jnp.float32(1.0))

    def fine(state_buffers, step_count):
        clock_delta = jnp.float32(1.0) / step_count.astype(jnp.float32)

        def one_step(step_no, current):
            return jnp.where(step_no < step_count, advance(current, clock_delta), current)

        return lax.fori_loop(0, STEPS_MAX, one_step, state_buffers)

    starts = [initial]
    coarse_ends = []
    for slab_no in range(SLABS):
        coarse_end = coarse(starts[slab_no])
        coarse_ends.append(coarse_end)
        starts.append(coarse_end)
    ends_now = coarse_ends
    for iter_no in range(ITERS):
        corrections = [fine(starts[slab_no], slab_steps[slab_no]) - coarse_ends[slab_no] for slab_no in range(SLABS)]
        new_starts = [initial]
        new_coarse = []
        ends_now = []
        for slab_no in range(SLABS):
            coarse_end = coarse(new_starts[slab_no])
            new_coarse.append(coarse_end)
            corrected = coarse_end + corrections[slab_no]
            ends_now.append(corrected)
            new_starts.append(corrected)
        starts = new_starts
        coarse_ends = new_coarse
    return jnp.stack(ends_now, 0)
```

```python
import functools

import jax
import jax.numpy as jnp
from jax import lax
from jax.experimental import pallas as pl
from jax.experimental.pallas import tpu as pltpu
from jax.sharding import PartitionSpec as P

STEPS_MAX = 8
STRIP = 16
LANES = 128
TABLE = 6 * STRIP
DRAG = TABLE + 8
GROUND = TABLE + 9
CODE_LEFT = TABLE + 10
CODE_RIGHT = TABLE + 11
MESH = pl.DeviceIdType.MESH


def roll(x, shift, axis):
    size = x.shape[axis]
    shift = shift % size
    return x if shift == 0 else pltpu.roll(x, shift, axis)


def column(row):
    pipes = row.shape[1]
    here = lax.broadcasted_iota(jnp.int32, (pipes, pipes), 0)
    there = lax.broadcasted_iota(jnp.int32, (pipes, pipes), 1)
    return jnp.sum(jnp.where(here == there, row, 0.0), axis=1, keepdims=True)


def gather_kernel(parts, slabs, x_ref, drag_ref, ground_ref, send_ref, recv_ref, steps_ref,
                  all_ref, count_ref, send_sem, recv_sem, step_send_sem, step_recv_sem):
    me = lax.axis_index("net")
    slab = lax.axis_index("tm")
    pipes = x_ref.shape[1]
    cells = x_ref.shape[2]
    slots = send_ref.shape[2]
    barrier = pltpu.get_barrier_semaphore()
    for off in range(1, parts):
        pl.semaphore_signal(barrier, inc=1, device_id={"net": lax.rem(me + off, parts)},
                            device_id_type=MESH)
    for off in range(1, slabs):
        pl.semaphore_signal(barrier, inc=1, device_id={"tm": lax.rem(slab + off, slabs)},
                            device_id_type=MESH)

    lane = lax.broadcasted_iota(jnp.int32, (pipes, LANES), 1)
    block = jnp.zeros((pipes, LANES), jnp.float32)
    for f in range(3):
        base = 2 * STRIP * f
        left = roll(x_ref[f, :, 0:LANES], base, 1)
        right = roll(x_ref[f, :, cells - LANES:cells], base + 2 * STRIP - LANES, 1)
        block = jnp.where((lane >= base) & (lane < base + STRIP), left, block)
        block = jnp.where((lane >= base + STRIP) & (lane < base + 2 * STRIP), right, block)
    pipe = lax.broadcasted_iota(jnp.int32, (pipes, slots), 0)
    slot = lax.broadcasted_iota(jnp.int32, (pipes, slots), 1) + (me // pipes) * slots
    code_left = jnp.zeros((pipes, slots), jnp.int32)
    code_right = jnp.zeros((pipes, slots), jnp.int32)
    for d in range(parts):
        listed = send_ref[0, d:d + 1, :]
        code_left = jnp.where(listed == pipe, slot + 8 * d, code_left)
        code_right = jnp.where(listed == pipe + pipes, slot + 8 * d, code_right)
    code_left = jnp.sum(code_left.astype(jnp.float32), axis=1, keepdims=True)
    code_right = jnp.sum(code_right.astype(jnp.float32), axis=1, keepdims=True)
    for at, value in ((DRAG, column(drag_ref[...].reshape(1, pipes))),
                      (GROUND, column(ground_ref[...].reshape(1, pipes))),
                      (CODE_LEFT, code_left), (CODE_RIGHT, code_right)):
        block = jnp.where(lane == at, value, block)
    mine = pl.ds(pl.multiple_of(me * pipes, pipes), pipes)
    all_ref[mine, :] = block
    for g in range(-(-parts // pipes)):
        rows = min(pipes, parts - g * pipes)
        all_ref[pl.ds(pl.multiple_of(me * pipes, pipes), rows),
                TABLE + g * slots:TABLE + (g + 1) * slots] = (
            recv_ref[0, g * pipes:g * pipes + rows, :].astype(jnp.float32))
    count_ref[slab] = jnp.full((8, LANES), steps_ref[0], jnp.int32)

    pl.semaphore_wait(barrier, parts - 1 + slabs - 1)
    copies = []
    for off in range(1, slabs):
        copies.append(pltpu.make_async_remote_copy(
            src_ref=count_ref.at[slab], dst_ref=count_ref.at[slab],
            send_sem=step_send_sem.at[off], recv_sem=step_recv_sem.at[off],
            device_id={"tm": lax.rem(slab + off, slabs)}, device_id_type=MESH))
    for off in range(1, parts):
        copies.append(pltpu.make_async_remote_copy(
            src_ref=all_ref.at[mine], dst_ref=all_ref.at[mine],
            send_sem=send_sem.at[off], recv_sem=recv_sem.at[off],
            device_id={"net": lax.rem(me + off, parts)}, device_id_type=MESH))
    for copy in copies:
        copy.start()
    for copy in copies:
        copy.wait()


def coarse_step(state, drag, cool, before, after, z=None):
    p, q, t = state
    zl, zr, tl, tr = (None,) * 4 if z is None else z
    a = before(p + q, zl)
    b = after(p - q, zr)
    return finish(a, b, q, t, 1.0, drag, cool, before, after, tl, tr)


def fine_step(state, h, drag, cool, before, after, z=None):
    p, q, t = state
    zl, zr, tl, tr = (None,) * 4 if z is None else z
    a = p + q
    b = p - q
    a = a - h * (a - before(a, zl))
    b = b - h * (b - after(b, zr))
    return finish(a, b, q, t, h, drag, cool, before, after, tl, tr)


def finish(a, b, q, t, h, drag, cool, before, after, tl, tr):
    r = 0.5 * (a - b)
    u = q / (1.0 + jnp.abs(q))
    flux = r / (1.0 + drag * jnp.abs(r))
    gain = jnp.maximum(u, 0.0) * (t - before(t, tl)) + jnp.minimum(u, 0.0) * (after(t, tr) - t)
    return 0.5 * (a + b), flux, (t - h * gain) * cool


def solve_kernel(parts, slabs, depth, x_ref, all_ref, steps_ref, out_ref,
                 deep_ref, u_ref, s_ref, v_ref, adj_ref, inv_ref, iu_ref, iv_ref, back_ref):
    me = lax.axis_index("net")
    slab = lax.axis_index("tm")
    pipes = x_ref.shape[1]
    cells = x_ref.shape[2]
    total = parts * pipes
    junctions = pipes // 2
    reach = slabs + STEPS_MAX - 1
    extra = depth - STRIP
    f32, bf16, i32 = jnp.float32, jnp.bfloat16, jnp.int32
    mine = pl.ds(pl.multiple_of(me * pipes, pipes), pipes)

    lane = lax.broadcasted_iota(i32, (pipes, LANES), 1)
    block = jnp.zeros((pipes, LANES), f32)
    for f in range(3):
        base = 2 * extra * f
        left = roll(x_ref[f, :, 0:LANES], base - STRIP, 1)
        right = roll(x_ref[f, :, cells - LANES:cells], base + extra - (LANES - depth), 1)
        block = jnp.where((lane >= base) & (lane < base + extra), left, block)
        block = jnp.where((lane >= base + extra) & (lane < base + 2 * extra), right, block)
    deep_ref[...] = jnp.zeros_like(deep_ref)
    deep_ref[mine, :] = block
    deep = deep_ref[...].T
    shallow = all_ref[...].T
    for f in range(3):
        base = 2 * STRIP * f
        near = 2 * extra * f
        s_ref[0, f, 0:STRIP, :] = shallow[base:base + STRIP]
        s_ref[0, f, STRIP:depth, :] = deep[near:near + extra]
        s_ref[0, f, depth:depth + extra, :] = deep[near + extra:near + 2 * extra]
        s_ref[0, f, depth + extra:2 * depth, :] = shallow[base + STRIP:base + 2 * STRIP]
    u_ref[0] = s_ref[0]
    v_ref[...] = s_ref[0]
    drag = shallow[DRAG:DRAG + 1]
    ground = shallow[GROUND:GROUND + 1]

    source = lax.broadcasted_iota(i32, (total, total), 0)
    target = lax.broadcasted_iota(i32, (total, total), 1)
    spread = ((source % pipes) == ((target // pipes) % pipes)).astype(f32).astype(bf16)
    table = shallow[TABLE:TABLE + 8]
    owner_of = lax.broadcasted_iota(i32, (8, total), 1) // pipes
    rows = jnp.concatenate([jnp.where(owner_of == d, table, 0.0) for d in range(parts)], 0)
    known = jnp.dot(rows.astype(bf16), spread, preferred_element_type=f32)
    place = lax.broadcasted_iota(i32, (8 * parts, total), 0)
    known = known + (junctions * (place // 8)).astype(f32)
    names = []
    for at in (CODE_LEFT, CODE_RIGHT):
        hit = place.astype(f32) == shallow[at:at + 1]
        names.append(jnp.sum(jnp.where(hit, known, 0.0), axis=0, keepdims=True))
    name = jnp.concatenate(names, 1)
    number = lax.broadcasted_iota(i32, (parts * junctions, 2 * total), 0).astype(f32)
    member = (number == name).astype(f32).astype(bf16)
    meets = lax.dot_general(member, member, (((0,), (0,)), ((), ())), preferred_element_type=f32)
    adj_ref[...] = meets.astype(bf16)
    inv_ref[...] = 1.0 / jnp.sum(meets, axis=0, keepdims=True)

    last = 2 * depth - 1
    row_at = lax.broadcasted_iota(i32, (2 * depth, total), 0)

    def before(x, z):
        return jnp.where(row_at == 0, z, roll(x, 1, 0))

    def after(x, z):
        return jnp.where(row_at == last, z, roll(x, -1, 0))

    def couple(states):
        count = len(states)
        height = -(-2 * count // 8) * 8
        at = lax.broadcasted_iota(i32, (height, 2 * total), 0)
        packed = jnp.zeros((height, 2 * total), f32)
        waves = []
        for n, (p, q, t) in enumerate(states):
            wave = jnp.concatenate(
                [p[0:1] - q[0:1], p[last:last + 1] + q[last:last + 1]], 1)
            waves.append(wave)
            warmth = jnp.concatenate([t[0:1], t[last:last + 1]], 1)
            packed = jnp.where(at == 2 * n, wave, packed)
            packed = jnp.where(at == 2 * n + 1, warmth, packed)
        high = packed.astype(bf16)
        rest = packed - high.astype(f32)
        mid = rest.astype(bf16)
        low = (rest - mid.astype(f32)).astype(bf16)
        adj = adj_ref[...]
        sums = (jnp.dot(low, adj, preferred_element_type=f32)
                + jnp.dot(mid, adj, preferred_element_type=f32)
                + jnp.dot(high, adj, preferred_element_type=f32))
        means = sums * inv_ref[...]
        ghosts = []
        for n in range(count):
            z = 2.0 * means[2 * n:2 * n + 1] - waves[n]
            th = means[2 * n + 1:2 * n + 2]
            ghosts.append((z[:, :total], z[:, total:], th[:, :total], th[:, total:]))
        return ghosts

    cool_one = 1.0 / (1.0 + ground)

    def coarse_strip(state):
        return coarse_step(state, drag, cool_one, before, after, couple([state])[0])

    def chain(n, carry):
        state = tuple(u_ref[n, f] for f in range(3))
        state = coarse_strip(state)
        for f in range(3):
            u_ref[n + 1, f] = state[f]
        return carry

    lax.fori_loop(0, slabs, chain, 0)
    for n in range(1, slabs):
        s_ref[n] = u_ref[n]
    hs, drags, cools = [], [], []
    for n in range(slabs):
        h = 1.0 / (jnp.zeros((1, total), f32) + steps_ref[n, 0, 0].astype(f32))
        hs.append(h)
        drags.append(h * drag)
        cools.append(1.0 / (1.0 + h * ground))

    def fine(m, carry):
        states = [tuple(s_ref[n, f] for f in range(3)) for n in range(slabs)]
        ghosts = couple(states)
        for n in range(slabs):
            @pl.when(m < steps_ref[n, 0, 0])
            def _():
                new = fine_step(states[n], hs[n], drags[n], cools[n], before, after, ghosts[n])
                for f in range(3):
                    s_ref[n, f] = new[f]
        return carry

    lax.fori_loop(0, STEPS_MAX, fine, 0)

    def correct(n, carry):
        state = coarse_strip(tuple(v_ref[f] for f in range(3)))
        for f in range(3):
            v_ref[f] = state[f] + (s_ref[n, f] - u_ref[n + 1, f])
        return carry

    lax.fori_loop(0, slab + 1, correct, 0)
    pieces = []
    for f in range(3):
        pieces.append(v_ref[f, 0:STRIP, :])
        pieces.append(v_ref[f, 2 * depth - STRIP:2 * depth, :])
    pieces.append(jnp.zeros((LANES - TABLE, total), f32))
    back_ref[...] = jnp.concatenate(pieces, 0).T

    for half in range(pipes // 8):
        span = pl.ds(half * 8, 8)
        own = pl.ds(pl.multiple_of(me * pipes + half * 8, 8), 8)
        params = all_ref[own, :]
        drag_c = jnp.broadcast_to(params[:, DRAG:DRAG + 1], (8, LANES))[:, 0:1]
        ground_c = params[:, GROUND:GROUND + 1]
        cool_c = 1.0 / (1.0 + ground_c)

        def left_of(x, z):
            return roll(x, 1, 1)

        def right_of(x, z):
            return roll(x, -1, 1)

        for f in range(3):
            iu_ref[f] = x_ref[f, span, :]
            iv_ref[f] = x_ref[f, span, :]

        def inner(n, carry):
            start = tuple(iu_ref[f] for f in range(3))
            count = steps_ref[n, 0, 0]
            h = 1.0 / (jnp.zeros((8, 1), f32) + count.astype(f32))
            drag_h = h * drag_c
            cool_h = 1.0 / (1.0 + h * ground_c)
            end = lax.fori_loop(
                0, count,
                lambda m, s: fine_step(s, h, drag_h, cool_h, left_of, right_of), start)
            guess = coarse_step(start, drag_c, cool_c, left_of, right_of)
            value = coarse_step(tuple(iv_ref[f] for f in range(3)), drag_c, cool_c,
                                left_of, right_of)
            for f in range(3):
                iu_ref[f] = guess[f]
                iv_ref[f] = value[f] + (end[f] - guess[f])
            return carry

        lax.fori_loop(0, slab + 1, inner, 0)
        ends = back_ref[own, :]
        lane8 = lax.broadcasted_iota(i32, (8, LANES), 1)
        for f in range(3):
            base = 2 * STRIP * f
            out_ref[0, f, span, :] = iv_ref[f]
            out_ref[0, f, span, 0:LANES] = jnp.where(
                lane8 < reach, roll(ends, -base, 1), iv_ref[f, :, 0:LANES])
            out_ref[0, f, span, cells - LANES:cells] = jnp.where(
                lane8 >= LANES - reach, roll(ends, LANES - 2 * STRIP - base, 1),
                iv_ref[f, :, cells - LANES:cells])


def body(parts, slabs, initial, wall_drag_factor, ground_exchange_rate, send_ends, recv_junction,
         slab_steps):
    pipes, cells = initial.shape[1:]
    total = parts * pipes
    depth = -(-2 * (slabs + STEPS_MAX - 1) // 8) * 8
    vmem = pl.BlockSpec(memory_space=pltpu.VMEM)
    smem = pl.BlockSpec(memory_space=pltpu.SMEM)
    gathered, counts = pl.pallas_call(
        functools.partial(gather_kernel, parts, slabs),
        out_shape=(jax.ShapeDtypeStruct((total, LANES), jnp.float32),
                   jax.ShapeDtypeStruct((slabs, 8, LANES), jnp.int32)),
        in_specs=[vmem] * 5 + [smem],
        out_specs=(vmem, vmem),
        scratch_shapes=[pltpu.SemaphoreType.DMA((parts,)), pltpu.SemaphoreType.DMA((parts,)),
                        pltpu.SemaphoreType.DMA((slabs,)), pltpu.SemaphoreType.DMA((slabs,))],
        compiler_params=pltpu.CompilerParams(collective_id=0, has_side_effects=True),
        name="gather_ends",
    )(initial, wall_drag_factor, ground_exchange_rate, send_ends, recv_junction, slab_steps)
    return pl.pallas_call(
        functools.partial(solve_kernel, parts, slabs, depth),
        out_shape=jax.ShapeDtypeStruct((1, 3, pipes, cells), jnp.float32),
        in_specs=[vmem, vmem, smem],
        out_specs=vmem,
        scratch_shapes=[
            pltpu.VMEM((total, LANES), jnp.float32),
            pltpu.VMEM((slabs + 1, 3, 2 * depth, total), jnp.float32),
            pltpu.VMEM((slabs, 3, 2 * depth, total), jnp.float32),
            pltpu.VMEM((3, 2 * depth, total), jnp.float32),
            pltpu.VMEM((2 * total, 2 * total), jnp.bfloat16),
            pltpu.VMEM((1, 2 * total), jnp.float32),
            pltpu.VMEM((3, 8, cells), jnp.float32),
            pltpu.VMEM((3, 8, cells), jnp.float32),
            pltpu.VMEM((total, LANES), jnp.float32),
        ],
        name="solve",
    )(initial, gathered, counts)


def solution(mesh):
    return jax.shard_map(
        functools.partial(body, mesh.shape["net"], mesh.shape["tm"]),
        mesh=mesh,
        in_specs=(
            P(None, "net", None),
            P("net"),
            P("net"),
            P("net", None, None),
            P("net", None, None),
            P("tm"),
        ),
        out_specs=P("tm", None, "net", None),
        check_vma=False,
    )
```

```python
import functools

import jax
import jax.numpy as jnp
from jax import lax
from jax.experimental import pallas as pl
from jax.experimental.pallas import tpu as pltpu
from jax.sharding import PartitionSpec as P

STEPS_MAX = 8
STEPS_MIN = 4
STRIP = 16
LANES = 128
TABLE = 6 * STRIP
DRAG = TABLE + 8
GROUND = TABLE + 9
CODE_LEFT = TABLE + 10
CODE_RIGHT = TABLE + 11
MESH = pl.DeviceIdType.MESH


def roll(x, shift, axis):
    size = x.shape[axis]
    shift = shift % size
    return x if shift == 0 else pltpu.roll(x, shift, axis)


def column(row):
    pipes = row.shape[1]
    here = lax.broadcasted_iota(jnp.int32, (pipes, pipes), 0)
    there = lax.broadcasted_iota(jnp.int32, (pipes, pipes), 1)
    return jnp.sum(jnp.where(here == there, row, 0.0), axis=1, keepdims=True)


def gather_kernel(parts, slabs, depth, x_ref, drag_ref, ground_ref, send_ref, recv_ref, steps_ref,
                  all_ref, count_ref, deep_ref, mid_ref, iu_ref, iv_ref, send_sem, recv_sem, step_send_sem, step_recv_sem):
    me = lax.axis_index("net")
    slab = lax.axis_index("tm")
    pipes = x_ref.shape[1]
    cells = x_ref.shape[2]
    slots = send_ref.shape[2]
    barrier = pltpu.get_barrier_semaphore()
    for off in range(1, parts):
        pl.semaphore_signal(barrier, inc=1, device_id={"net": lax.rem(me + off, parts)},
                            device_id_type=MESH)
    for off in range(1, slabs):
        pl.semaphore_signal(barrier, inc=1, device_id={"tm": lax.rem(slab + off, slabs)},
                            device_id_type=MESH)

    lane = lax.broadcasted_iota(jnp.int32, (pipes, LANES), 1)
    block = jnp.zeros((pipes, LANES), jnp.float32)
    for f in range(3):
        base = 2 * STRIP * f
        left = roll(x_ref[f, :, 0:LANES], base, 1)
        right = roll(x_ref[f, :, cells - LANES:cells], base + 2 * STRIP - LANES, 1)
        block = jnp.where((lane >= base) & (lane < base + STRIP), left, block)
        block = jnp.where((lane >= base + STRIP) & (lane < base + 2 * STRIP), right, block)
    pipe = lax.broadcasted_iota(jnp.int32, (pipes, slots), 0)
    slot = lax.broadcasted_iota(jnp.int32, (pipes, slots), 1) + (me // pipes) * slots
    code_left = jnp.zeros((pipes, slots), jnp.int32)
    code_right = jnp.zeros((pipes, slots), jnp.int32)
    for d in range(parts):
        listed = send_ref[0, d:d + 1, :]
        code_left = jnp.where(listed == pipe, slot + 8 * d, code_left)
        code_right = jnp.where(listed == pipe + pipes, slot + 8 * d, code_right)
    code_left = jnp.sum(code_left.astype(jnp.float32), axis=1, keepdims=True)
    code_right = jnp.sum(code_right.astype(jnp.float32), axis=1, keepdims=True)
    for at, value in ((DRAG, column(drag_ref[...].reshape(1, pipes))),
                      (GROUND, column(ground_ref[...].reshape(1, pipes))),
                      (CODE_LEFT, code_left), (CODE_RIGHT, code_right)):
        block = jnp.where(lane == at, value, block)
    mine = pl.ds(pl.multiple_of(me * pipes, pipes), pipes)
    all_ref[mine, :] = block
    for g in range(-(-parts // pipes)):
        rows = min(pipes, parts - g * pipes)
        all_ref[pl.ds(pl.multiple_of(me * pipes, pipes), rows),
                TABLE + g * slots:TABLE + (g + 1) * slots] = (
            recv_ref[0, g * pipes:g * pipes + rows, :].astype(jnp.float32))
    count_ref[slab] = jnp.full((8, LANES), steps_ref[0], jnp.int32)

    pl.semaphore_wait(barrier, parts - 1 + slabs - 1)
    copies = []
    for off in range(1, slabs):
        copies.append(pltpu.make_async_remote_copy(
            src_ref=count_ref.at[slab], dst_ref=count_ref.at[slab],
            send_sem=step_send_sem.at[off], recv_sem=step_recv_sem.at[off],
            device_id={"tm": lax.rem(slab + off, slabs)}, device_id_type=MESH))
    for off in range(1, parts):
        copies.append(pltpu.make_async_remote_copy(
            src_ref=all_ref.at[mine], dst_ref=all_ref.at[mine],
            send_sem=send_sem.at[off], recv_sem=recv_sem.at[off],
            device_id={"net": lax.rem(me + off, parts)}, device_id_type=MESH))
    for copy in copies:
        copy.start()

    extra = depth - STRIP
    block = jnp.zeros((pipes, LANES), jnp.float32)
    for f in range(3):
        base = 2 * extra * f
        left = roll(x_ref[f, :, 0:LANES], base - STRIP, 1)
        right = roll(x_ref[f, :, cells - LANES:cells], base + extra - (LANES - depth), 1)
        block = jnp.where((lane >= base) & (lane < base + extra), left, block)
        block = jnp.where((lane >= base + extra) & (lane < base + 2 * extra), right, block)
    deep_ref[...] = block
    for copy in copies[:slabs - 1]:
        copy.wait()

    def left_of(x, z):
        return roll(x, 1, 1)

    def right_of(x, z):
        return roll(x, -1, 1)

    for half in range(pipes // 8):
        span = pl.ds(half * 8, 8)
        own = pl.ds(pl.multiple_of(me * pipes + half * 8, 8), 8)
        params = all_ref[own, :]
        drag_c = params[:, DRAG:DRAG + 1]
        ground_c = params[:, GROUND:GROUND + 1]
        cool_c = 1.0 / (1.0 + ground_c)
        for f in range(3):
            iu_ref[f] = x_ref[f, span, :]
            iv_ref[f] = x_ref[f, span, :]

        def inner(n, carry):
            start = tuple(iu_ref[f] for f in range(3))
            count = count_ref[n]
            h = 1.0 / count[:, 0:1].astype(jnp.float32)
            drag_h = h * drag_c
            cool_h = 1.0 / (1.0 + h * ground_c)

            def step(m, s):
                return fine_step(s, h, drag_h, cool_h, left_of, right_of)

            def maybe(m, s):
                live = jnp.concatenate([m < count] * (cells // LANES), 1)
                return tuple(jnp.where(live, a, b) for a, b in zip(step(m, s), s))

            end = lax.fori_loop(0, STEPS_MIN, step, start)
            end = lax.fori_loop(STEPS_MIN, STEPS_MAX, maybe, end)
            guess = coarse_step(start, drag_c, cool_c, left_of, right_of)
            value = coarse_step(tuple(iv_ref[f] for f in range(3)), drag_c, cool_c,
                                left_of, right_of)
            for f in range(3):
                iu_ref[f] = guess[f]
                iv_ref[f] = value[f] + (end[f] - guess[f])
            return carry

        lax.fori_loop(0, slab + 1, inner, 0)
        for f in range(3):
            mid_ref[0, f, span, :] = iv_ref[f]
    for copy in copies[slabs - 1:]:
        copy.wait()


def coarse_step(state, drag, cool, before, after, z=None):
    p, q, t = state
    zl, zr, tl, tr = (None,) * 4 if z is None else z
    a = before(p + q, zl)
    b = after(p - q, zr)
    return finish(0.5 * (a + b), 0.5 * (a - b), q, t, None, drag, cool, before, after, tl, tr)


def fine_step(state, h, drag, cool, before, after, z=None):
    p, q, t = state
    zl, zr, tl, tr = (None,) * 4 if z is None else z
    a = p + q
    b = p - q
    da = a - before(a, zl)
    db = b - after(b, zr)
    half = 0.5 * h
    return finish(p - half * (da + db), q - half * (da - db), q, t, h, drag, cool, before, after,
                  tl, tr)


def finish(p, r, q, t, h, drag, cool, before, after, tl, tr):
    slow = 1.0 + jnp.abs(q)
    dragged = 1.0 + drag * jnp.abs(r)
    inverse = 1.0 / (slow * dragged)
    u = q * (dragged * inverse)
    gain = jnp.maximum(u, 0.0) * (t - before(t, tl)) + jnp.minimum(u, 0.0) * (after(t, tr) - t)
    if h is not None:
        gain = h * gain
    return p, r * (slow * inverse), (t - gain) * cool


def solve_kernel(parts, slabs, depth, mid_ref, own_ref, all_ref, steps_ref, out_ref,
                 deep_ref, u_ref, s_ref, v_ref, adj_ref, inv_ref, back_ref):
    me = lax.axis_index("net")
    slab = lax.axis_index("tm")
    pipes = mid_ref.shape[2]
    cells = mid_ref.shape[3]
    total = parts * pipes
    junctions = pipes // 2
    reach = slabs + STEPS_MAX - 1
    extra = depth - STRIP
    f32, bf16, i32 = jnp.float32, jnp.bfloat16, jnp.int32
    mine = pl.ds(pl.multiple_of(me * pipes, pipes), pipes)

    deep_ref[...] = jnp.zeros_like(deep_ref)
    deep_ref[mine, :] = own_ref[...]
    deep = deep_ref[...].T
    shallow = all_ref[...].T
    for f in range(3):
        base = 2 * STRIP * f
        near = 2 * extra * f
        s_ref[0, f, 0:STRIP, :] = shallow[base:base + STRIP]
        s_ref[0, f, STRIP:depth, :] = deep[near:near + extra]
        s_ref[0, f, depth:depth + extra, :] = deep[near + extra:near + 2 * extra]
        s_ref[0, f, depth + extra:2 * depth, :] = shallow[base + STRIP:base + 2 * STRIP]
    drag = shallow[DRAG:DRAG + 1]
    ground = shallow[GROUND:GROUND + 1]

    source = lax.broadcasted_iota(i32, (total, total), 0)
    target = lax.broadcasted_iota(i32, (total, total), 1)
    spread = ((source % pipes) == ((target // pipes) % pipes)).astype(f32).astype(bf16)
    table = shallow[TABLE:TABLE + 8]
    owner_of = lax.broadcasted_iota(i32, (8, total), 1) // pipes
    rows = jnp.concatenate([jnp.where(owner_of == d, table, 0.0) for d in range(parts)], 0)
    known = jnp.dot(rows.astype(bf16), spread, preferred_element_type=f32)
    place = lax.broadcasted_iota(i32, (8 * parts, total), 0)
    known = known + (junctions * (place // 8)).astype(f32)
    names = []
    for at in (CODE_LEFT, CODE_RIGHT):
        hit = place.astype(f32) == shallow[at:at + 1]
        names.append(jnp.sum(jnp.where(hit, known, 0.0), axis=0, keepdims=True))
    name = jnp.concatenate(names, 1)
    number = lax.broadcasted_iota(i32, (parts * junctions, 2 * total), 0).astype(f32)
    member = (number == name).astype(f32).astype(bf16)
    meets = lax.dot_general(member, member, (((0,), (0,)), ((), ())), preferred_element_type=f32)
    adj_ref[...] = meets.astype(bf16)
    inv_ref[...] = 1.0 / jnp.sum(meets, axis=0, keepdims=True)

    last = 2 * depth - 1
    row_at = lax.broadcasted_iota(i32, (2 * depth, total), 0)

    def before(x, z):
        return jnp.where(row_at == 0, z, roll(x, 1, 0))

    def after(x, z):
        return jnp.where(row_at == last, z, roll(x, -1, 0))

    def couple(states):
        count = len(states)
        height = -(-2 * count // 8) * 8
        at = lax.broadcasted_iota(i32, (height, 2 * total), 0)
        packed = jnp.zeros((height, 2 * total), f32)
        waves = []
        for n, (p, q, t) in enumerate(states):
            wave = jnp.concatenate(
                [p[0:1] - q[0:1], p[last:last + 1] + q[last:last + 1]], 1)
            waves.append(wave)
            warmth = jnp.concatenate([t[0:1], t[last:last + 1]], 1)
            packed = jnp.where(at == 2 * n, wave, packed)
            packed = jnp.where(at == 2 * n + 1, warmth, packed)
        high = packed.astype(bf16)
        rest = packed - high.astype(f32)
        mid = rest.astype(bf16)
        low = (rest - mid.astype(f32)).astype(bf16)
        adj = adj_ref[...]
        sums = (jnp.dot(low, adj, preferred_element_type=f32)
                + jnp.dot(mid, adj, preferred_element_type=f32)
                + jnp.dot(high, adj, preferred_element_type=f32))
        means = sums * inv_ref[...]
        ghosts = []
        for n in range(count):
            z = 2.0 * means[2 * n:2 * n + 1] - waves[n]
            th = means[2 * n + 1:2 * n + 2]
            ghosts.append((z[:, :total], z[:, total:], th[:, :total], th[:, total:]))
        return ghosts

    cool_one = 1.0 / (1.0 + ground)
    hs, drags, cools = [], [], []
    for n in range(slabs):
        h = 1.0 / (jnp.zeros((1, total), f32) + steps_ref[n, 0, 0].astype(f32))
        hs.append(h)
        drags.append(h * drag)
        cools.append(1.0 / (1.0 + h * ground))

    def coarse(state, ghosts):
        return coarse_step(state, drag, cool_one, before, after, ghosts)

    def load(ref, n):
        return tuple(ref[n, f] for f in range(3))

    def store(ref, n, state):
        for f in range(3):
            ref[n, f] = state[f]

    def advance(n, m, state, ghosts):
        new = fine_step(state, hs[n], drags[n], cools[n], before, after, ghosts)
        if isinstance(m, int) and m < STEPS_MIN:
            return new
        live = m < steps_ref[n, 0, 0]
        return tuple(jnp.where(live, a, b) for a, b in zip(new, state))

    for t in range(slabs):
        states = [load(s_ref, n) for n in range(t + 1)]
        ghosts = couple(states)
        guess = coarse(states[t], ghosts[t])
        store(u_ref, t, guess)
        if t + 1 < slabs:
            store(s_ref, t + 1, guess)
        for n in range(t + 1):
            store(s_ref, n, advance(n, t - n, states[n], ghosts[n]))

    def stage(t, carry):
        states = [load(s_ref, n) for n in range(slabs)]
        ghosts = couple(states)
        for n in range(slabs):
            store(s_ref, n, advance(n, t - n, states[n], ghosts[n]))
        return carry

    lax.fori_loop(slabs, STEPS_MAX, stage, 0)
    value = load(s_ref, 0)
    store(v_ref, 0, value)
    for t in range(STEPS_MAX, STEPS_MAX + slabs - 1):
        first = t - STEPS_MAX + 1
        states = [load(s_ref, n) for n in range(first, slabs)]
        ghosts = couple([value] + states)
        guess = load(u_ref, first)
        ends = [advance(n, t - n, states[n - first], ghosts[n - first + 1])
                for n in range(first, slabs)]
        for n in range(first + 1, slabs):
            store(s_ref, n, ends[n - first])
        value = tuple(g + (e - u) for g, e, u in zip(coarse(value, ghosts[0]), ends[0], guess))
        store(v_ref, first, value)
    pieces = []
    for f in range(3):
        pieces.append(v_ref[slab, f, 0:STRIP, :])
        pieces.append(v_ref[slab, f, 2 * depth - STRIP:2 * depth, :])
    pieces.append(jnp.zeros((LANES - TABLE, total), f32))
    back_ref[...] = jnp.concatenate(pieces, 0).T

    ends = back_ref[mine, :]
    lane = lax.broadcasted_iota(i32, (pipes, LANES), 1)
    for f in range(3):
        base = 2 * STRIP * f
        out_ref[0, f, :, LANES:cells - LANES] = mid_ref[0, f, :, LANES:cells - LANES]
        out_ref[0, f, :, 0:LANES] = jnp.where(
            lane < reach, roll(ends, -base, 1), mid_ref[0, f, :, 0:LANES])
        out_ref[0, f, :, cells - LANES:cells] = jnp.where(
            lane >= LANES - reach, roll(ends, LANES - 2 * STRIP - base, 1),
            mid_ref[0, f, :, cells - LANES:cells])


def body(parts, slabs, initial, wall_drag_factor, ground_exchange_rate, send_ends, recv_junction,
         slab_steps):
    pipes, cells = initial.shape[1:]
    total = parts * pipes
    depth = -(-2 * (slabs + STEPS_MAX - 1) // 8) * 8
    vmem = pl.BlockSpec(memory_space=pltpu.VMEM)
    smem = pl.BlockSpec(memory_space=pltpu.SMEM)
    gathered, counts, own, mid = pl.pallas_call(
        functools.partial(gather_kernel, parts, slabs, depth),
        out_shape=(jax.ShapeDtypeStruct((total, LANES), jnp.float32),
                   jax.ShapeDtypeStruct((slabs, 8, LANES), jnp.int32),
                   jax.ShapeDtypeStruct((pipes, LANES), jnp.float32),
                   jax.ShapeDtypeStruct((1, 3, pipes, cells), jnp.float32)),
        in_specs=[vmem] * 5 + [smem],
        out_specs=(vmem,) * 4,
        scratch_shapes=[pltpu.VMEM((3, 8, cells), jnp.float32),
                        pltpu.VMEM((3, 8, cells), jnp.float32),
                        pltpu.SemaphoreType.DMA((parts,)), pltpu.SemaphoreType.DMA((parts,)),
                        pltpu.SemaphoreType.DMA((slabs,)), pltpu.SemaphoreType.DMA((slabs,))],
        compiler_params=pltpu.CompilerParams(collective_id=0, has_side_effects=True),
        name="gather_ends",
    )(initial, wall_drag_factor, ground_exchange_rate, send_ends, recv_junction, slab_steps)
    return pl.pallas_call(
        functools.partial(solve_kernel, parts, slabs, depth),
        out_shape=jax.ShapeDtypeStruct((1, 3, pipes, cells), jnp.float32),
        in_specs=[vmem, vmem, vmem, smem],
        out_specs=vmem,
        scratch_shapes=[
            pltpu.VMEM((total, LANES), jnp.float32),
            pltpu.VMEM((slabs, 3, 2 * depth, total), jnp.float32),
            pltpu.VMEM((slabs, 3, 2 * depth, total), jnp.float32),
            pltpu.VMEM((slabs, 3, 2 * depth, total), jnp.float32),
            pltpu.VMEM((2 * total, 2 * total), jnp.bfloat16),
            pltpu.VMEM((1, 2 * total), jnp.float32),
            pltpu.VMEM((total, LANES), jnp.float32),
        ],
        name="solve",
    )(mid, own, gathered, counts)


def solution(mesh):
    return jax.shard_map(
        functools.partial(body, mesh.shape["net"], mesh.shape["tm"]),
        mesh=mesh,
        in_specs=(
            P(None, "net", None),
            P("net"),
            P("net"),
            P("net", None, None),
            P("net", None, None),
            P("tm"),
        ),
        out_specs=P("tm", None, "net", None),
        check_vma=False,
    )
```

```python
import functools

import jax
import jax.numpy as jnp
from jax import lax
from jax.experimental import pallas as pl
from jax.experimental.pallas import tpu as pltpu
from jax.sharding import PartitionSpec as P

STEPS_MAX = 8
STEPS_MIN = 4
STRIP = 16
LANES = 128
TABLE = 6 * STRIP
PAD = 8
HALO = 16
DRAG = TABLE + 8
GROUND = TABLE + 9
CODE_LEFT = TABLE + 10
CODE_RIGHT = TABLE + 11
MESH = pl.DeviceIdType.MESH


def roll(x, shift, axis):
    size = x.shape[axis]
    shift = shift % size
    return x if shift == 0 else pltpu.roll(x, shift, axis)


def column(row):
    pipes = row.shape[1]
    here = lax.broadcasted_iota(jnp.int32, (pipes, pipes), 0)
    there = lax.broadcasted_iota(jnp.int32, (pipes, pipes), 1)
    return jnp.sum(jnp.where(here == there, row, 0.0), axis=1, keepdims=True)


def sweep(source, targets, rows, chunk, h, drag, cool, live=None):
    for low in range(PAD, PAD + rows, chunk):
        here, prior, coming = (pl.ds(low + off, chunk) for off in (0, -1, 1))
        a, b, t = (source[f, here, :] for f in range(3))
        a_prior, t_prior = source[0, prior, :], source[2, prior, :]
        b_coming, t_coming = source[1, coming, :], source[2, coming, :]
        q = 0.5 * (a - b)
        if h is None:
            ahead, back = a_prior, b_coming
        else:
            ahead, back = a - h * (a - a_prior), b - h * (b - b_coming)
        p = 0.5 * (ahead + back)
        r = 0.5 * (ahead - back)
        slow = 1.0 + jnp.abs(q)
        dragged = 1.0 + drag * jnp.abs(r)
        inverse = 1.0 / (slow * dragged)
        flux = r * (slow * inverse)
        u = q * (dragged * inverse)
        gain = jnp.maximum(u, 0.0) * (t - t_prior) + jnp.minimum(u, 0.0) * (t_coming - t)
        if h is not None:
            gain = h * gain
        new = (p + flux, p - flux, (t - gain) * cool)
        if live is not None:
            new = tuple(jnp.where(live, x, y) for x, y in zip(new, (a, b, t)))
        for target in targets:
            for f in range(3):
                target[f, here, :] = new[f]


def gather_kernel(parts, slabs, depth, x_ref, drag_ref, ground_ref, send_ref, recv_ref, steps_ref,
                  all_ref, count_ref, deep_ref, mid_ref, fold_ref, send_sem, recv_sem, step_send_sem, step_recv_sem):
    me = lax.axis_index("net")
    slab = lax.axis_index("tm")
    pipes = x_ref.shape[1]
    cells = x_ref.shape[2]
    slots = send_ref.shape[2]
    barrier = pltpu.get_barrier_semaphore()
    for off in range(1, parts):
        pl.semaphore_signal(barrier, inc=1, device_id={"net": lax.rem(me + off, parts)},
                            device_id_type=MESH)
    for off in range(1, slabs):
        pl.semaphore_signal(barrier, inc=1, device_id={"tm": lax.rem(slab + off, slabs)},
                            device_id_type=MESH)

    lane = lax.broadcasted_iota(jnp.int32, (pipes, LANES), 1)
    block = jnp.zeros((pipes, LANES), jnp.float32)
    for f in range(3):
        base = 2 * STRIP * f
        left = roll(x_ref[f, :, 0:LANES], base, 1)
        right = roll(x_ref[f, :, cells - LANES:cells], base + 2 * STRIP - LANES, 1)
        block = jnp.where((lane >= base) & (lane < base + STRIP), left, block)
        block = jnp.where((lane >= base + STRIP) & (lane < base + 2 * STRIP), right, block)
    pipe = lax.broadcasted_iota(jnp.int32, (pipes, slots), 0)
    slot = lax.broadcasted_iota(jnp.int32, (pipes, slots), 1) + (me // pipes) * slots
    code_left = jnp.zeros((pipes, slots), jnp.int32)
    code_right = jnp.zeros((pipes, slots), jnp.int32)
    for d in range(parts):
        listed = send_ref[0, d:d + 1, :]
        code_left = jnp.where(listed == pipe, slot + 8 * d, code_left)
        code_right = jnp.where(listed == pipe + pipes, slot + 8 * d, code_right)
    code_left = jnp.sum(code_left.astype(jnp.float32), axis=1, keepdims=True)
    code_right = jnp.sum(code_right.astype(jnp.float32), axis=1, keepdims=True)
    for at, value in ((DRAG, column(drag_ref[...].reshape(1, pipes))),
                      (GROUND, column(ground_ref[...].reshape(1, pipes))),
                      (CODE_LEFT, code_left), (CODE_RIGHT, code_right)):
        block = jnp.where(lane == at, value, block)
    mine = pl.ds(pl.multiple_of(me * pipes, pipes), pipes)
    all_ref[mine, :] = block
    for g in range(-(-parts // pipes)):
        rows = min(pipes, parts - g * pipes)
        all_ref[pl.ds(pl.multiple_of(me * pipes, pipes), rows),
                TABLE + g * slots:TABLE + (g + 1) * slots] = (
            recv_ref[0, g * pipes:g * pipes + rows, :].astype(jnp.float32))
    count_ref[slab] = jnp.full((8, LANES), steps_ref[0], jnp.int32)

    segments = cells // LANES
    rows = LANES + 2 * HALO
    fold_ref[:, :, 0:PAD, :] = jnp.zeros((5, 3, PAD, LANES), jnp.float32)
    fold_ref[:, :, PAD + rows:, :] = jnp.zeros((5, 3, PAD, LANES), jnp.float32)
    turned = [jnp.concatenate([x_ref[f, :, LANES * c:LANES * (c + 1)] for c in range(segments)],
                              0).T for f in range(3)]
    turned = (turned[0] + turned[1], turned[0] - turned[1], turned[2])
    for f in range(3):
        whole = jnp.concatenate([roll(turned[f][LANES - HALO:], pipes, 1), turned[f],
                                 roll(turned[f][:HALO], -pipes, 1)], 0)
        fold_ref[0, f, PAD:PAD + rows, :] = whole
        fold_ref[1, f, PAD:PAD + rows, :] = whole

    pl.semaphore_wait(barrier, parts - 1 + slabs - 1)
    copies = []
    for off in range(1, slabs):
        copies.append(pltpu.make_async_remote_copy(
            src_ref=count_ref.at[slab], dst_ref=count_ref.at[slab],
            send_sem=step_send_sem.at[off], recv_sem=step_recv_sem.at[off],
            device_id={"tm": lax.rem(slab + off, slabs)}, device_id_type=MESH))
    for off in range(1, parts):
        copies.append(pltpu.make_async_remote_copy(
            src_ref=all_ref.at[mine], dst_ref=all_ref.at[mine],
            send_sem=send_sem.at[off], recv_sem=recv_sem.at[off],
            device_id={"net": lax.rem(me + off, parts)}, device_id_type=MESH))
    for copy in copies:
        copy.start()

    extra = depth - STRIP
    block = jnp.zeros((pipes, LANES), jnp.float32)
    for f in range(3):
        base = 2 * extra * f
        left = roll(x_ref[f, :, 0:LANES], base - STRIP, 1)
        right = roll(x_ref[f, :, cells - LANES:cells], base + extra - (LANES - depth), 1)
        block = jnp.where((lane >= base) & (lane < base + extra), left, block)
        block = jnp.where((lane >= base + extra) & (lane < base + 2 * extra), right, block)
    deep_ref[...] = block
    for copy in copies[:slabs - 1]:
        copy.wait()

    own_pipe = lane % pipes == lax.broadcasted_iota(jnp.int32, (pipes, LANES), 0)

    def in_lanes(ref):
        return jnp.sum(jnp.where(own_pipe, column(ref[...].reshape(1, pipes)), 0.0), axis=0,
                       keepdims=True)

    drag = in_lanes(drag_ref)
    ground = in_lanes(ground_ref)
    cool = 1.0 / (1.0 + ground)
    start, value, guess, one, two = (fold_ref.at[k] for k in range(5))
    chunk = 40

    def inner(n, carry):
        count = count_ref[n][0:1]
        h = 1.0 / count.astype(jnp.float32)
        drag_h = h * drag
        cool_h = 1.0 / (1.0 + h * ground)
        sweep(start, [guess], rows, chunk, None, drag, cool)
        sweep(start, [one], rows, chunk, h, drag_h, cool_h)
        for source, target in ((one, two), (two, one), (one, two)):
            sweep(source, [target], rows, chunk, h, drag_h, cool_h)

        def pair(k, c):
            m = STEPS_MIN + 2 * k
            sweep(two, [one], rows, chunk, h, drag_h, cool_h, m < count)
            sweep(one, [two], rows, chunk, h, drag_h, cool_h, m + 1 < count)
            return c

        lax.fori_loop(0, (STEPS_MAX - STEPS_MIN) // 2, pair, 0)
        sweep(value, [one], rows, chunk, None, drag, cool)
        for low in range(PAD, PAD + rows, chunk):
            part = pl.ds(low, chunk)
            for f in range(3):
                coarse = guess[f, part, :]
                value[f, part, :] = one[f, part, :] + (two[f, part, :] - coarse)
                start[f, part, :] = coarse
        return carry

    lax.fori_loop(0, slab + 1, inner, 0)
    middle = pl.ds(PAD + HALO, LANES)
    a, b, t = (value[f, middle, :] for f in range(3))
    for f, x in enumerate((0.5 * (a + b), 0.5 * (a - b), t)):
        back = x.T
        for c in range(segments):
            mid_ref[0, f, :, LANES * c:LANES * (c + 1)] = back[pipes * c:pipes * (c + 1)]
    for copy in copies[slabs - 1:]:
        copy.wait()


def solve_kernel(parts, slabs, depth, mid_ref, own_ref, all_ref, steps_ref, out_ref,
                 deep_ref, u_ref, s_ref, v_ref, adj_ref, inv_ref, back_ref):
    me = lax.axis_index("net")
    slab = lax.axis_index("tm")
    pipes = mid_ref.shape[2]
    cells = mid_ref.shape[3]
    total = parts * pipes
    junctions = pipes // 2
    reach = slabs + STEPS_MAX - 1
    extra = depth - STRIP
    f32, bf16, i32 = jnp.float32, jnp.bfloat16, jnp.int32
    mine = pl.ds(pl.multiple_of(me * pipes, pipes), pipes)

    deep_ref[...] = jnp.zeros_like(deep_ref)
    deep_ref[mine, :] = own_ref[...]
    deep = deep_ref[...].T
    shallow = all_ref[...].T
    rows = 2 * depth
    edge = PAD + rows
    ends = []
    for f in range(3):
        base = 2 * STRIP * f
        near = 2 * extra * f
        ends.append(jnp.concatenate([
            shallow[base:base + STRIP], deep[near:near + 2 * extra],
            shallow[base + STRIP:base + 2 * STRIP]], 0))
    for f, x in enumerate((ends[0] + ends[1], ends[0] - ends[1], ends[2])):
        s_ref[0, 0, f, PAD:edge, :] = x
    drag = shallow[DRAG:DRAG + 1]
    ground = shallow[GROUND:GROUND + 1]

    source = lax.broadcasted_iota(i32, (total, total), 0)
    target = lax.broadcasted_iota(i32, (total, total), 1)
    spread = ((source % pipes) == ((target // pipes) % pipes)).astype(f32).astype(bf16)
    table = shallow[TABLE:TABLE + 8]
    owner_of = lax.broadcasted_iota(i32, (8, total), 1) // pipes
    listed = jnp.concatenate([jnp.where(owner_of == d, table, 0.0) for d in range(parts)], 0)
    known = jnp.dot(listed.astype(bf16), spread, preferred_element_type=f32)
    place = lax.broadcasted_iota(i32, (8 * parts, total), 0)
    known = known + (junctions * (place // 8)).astype(f32)
    names = []
    for at in (CODE_LEFT, CODE_RIGHT):
        hit = place.astype(f32) == shallow[at:at + 1]
        names.append(jnp.sum(jnp.where(hit, known, 0.0), axis=0, keepdims=True))
    name = jnp.concatenate(names, 1)
    number = lax.broadcasted_iota(i32, (parts * junctions, 2 * total), 0).astype(f32)
    member = (number == name).astype(f32).astype(bf16)
    meets = lax.dot_general(member, member, (((0,), (0,)), ((), ())), preferred_element_type=f32)
    adj_ref[...] = meets.astype(bf16)
    inv_ref[...] = 1.0 / jnp.sum(meets, axis=0, keepdims=True)

    def couple(states):
        count = len(states)
        height = -(-2 * count // 8) * 8
        at = lax.broadcasted_iota(i32, (height, 2 * total), 0)
        packed = jnp.zeros((height, 2 * total), f32)
        waves = []
        for n, state in enumerate(states):
            wave = jnp.concatenate(
                [state[1, PAD:PAD + 1, :], state[0, edge - 1:edge, :]], 1)
            waves.append(wave)
            warmth = jnp.concatenate(
                [state[2, PAD:PAD + 1, :], state[2, edge - 1:edge, :]], 1)
            packed = jnp.where(at == 2 * n, wave, packed)
            packed = jnp.where(at == 2 * n + 1, warmth, packed)
        high = packed.astype(bf16)
        rest = packed - high.astype(f32)
        mid = rest.astype(bf16)
        low = (rest - mid.astype(f32)).astype(bf16)
        adj = adj_ref[...]
        sums = (jnp.dot(low, adj, preferred_element_type=f32)
                + jnp.dot(mid, adj, preferred_element_type=f32)
                + jnp.dot(high, adj, preferred_element_type=f32))
        means = sums * inv_ref[...]
        for n, state in enumerate(states):
            z = 2.0 * means[2 * n:2 * n + 1] - waves[n]
            th = means[2 * n + 1:2 * n + 2]
            state[0, PAD - 1:PAD, :] = z[:, :total]
            state[1, edge:edge + 1, :] = z[:, total:]
            state[2, PAD - 1:PAD, :] = th[:, :total]
            state[2, edge:edge + 1, :] = th[:, total:]

    cool_one = 1.0 / (1.0 + ground)
    hs, drags, cools = [], [], []
    for n in range(slabs):
        h = 1.0 / (jnp.zeros((1, total), f32) + steps_ref[n, 0, 0].astype(f32))
        hs.append(h)
        drags.append(h * drag)
        cools.append(1.0 / (1.0 + h * ground))

    chunk = rows // 2
    last = STEPS_MAX + slabs - 2

    def fine(n, m):
        return s_ref.at[m % 2, n]

    def advance(n, m, also=()):
        live = None if m < STEPS_MIN else m < steps_ref[n, 0, 0]
        sweep(fine(n, m), [fine(n, m + 1), *also], rows, chunk, hs[n], drags[n], cools[n], live)

    for t in range(last + 1):
        active = [n for n in range(slabs) if 0 <= t - n < STEPS_MAX]
        states = [fine(n, t - n) for n in active]
        first = t - STEPS_MAX + 1
        if first >= 1:
            value = v_ref.at[first - 1]
            states.append(value)
        couple(states)
        if t < slabs:
            targets = [u_ref.at[t]] + ([fine(t + 1, 0)] if t + 1 < slabs else [])
            sweep(fine(t, 0), targets, rows, chunk, None, drag, cool_one)
        for n in active:
            advance(n, t - n, [v_ref.at[0]] if n == 0 and t == STEPS_MAX - 1 else [])
        if first >= 1:
            sweep(value, [v_ref.at[first]], rows, chunk, None, drag, cool_one)
            for f in range(3):
                v_ref[first, f, PAD:edge, :] = v_ref[first, f, PAD:edge, :] + (
                    s_ref[0, first, f, PAD:edge, :] - u_ref[first, f, PAD:edge, :])
    pieces = []
    for span in (pl.ds(PAD, STRIP), pl.ds(edge - STRIP, STRIP)):
        a, b, t = (v_ref[slab, f, span, :] for f in range(3))
        pieces.append((0.5 * (a + b), 0.5 * (a - b), t))
    pieces = [side[f] for f in range(3) for side in pieces]
    pieces.append(jnp.zeros((LANES - TABLE, total), f32))
    back_ref[...] = jnp.concatenate(pieces, 0).T
    ends = back_ref[mine, :]
    lane = lax.broadcasted_iota(i32, (pipes, LANES), 1)
    for f in range(3):
        base = 2 * STRIP * f
        out_ref[0, f, :, LANES:cells - LANES] = mid_ref[0, f, :, LANES:cells - LANES]
        out_ref[0, f, :, 0:LANES] = jnp.where(
            lane < reach, roll(ends, -base, 1), mid_ref[0, f, :, 0:LANES])
        out_ref[0, f, :, cells - LANES:cells] = jnp.where(
            lane >= LANES - reach, roll(ends, LANES - 2 * STRIP - base, 1),
            mid_ref[0, f, :, cells - LANES:cells])


def body(parts, slabs, initial, wall_drag_factor, ground_exchange_rate, send_ends, recv_junction,
         slab_steps):
    pipes, cells = initial.shape[1:]
    total = parts * pipes
    depth = -(-2 * (slabs + STEPS_MAX - 1) // 8) * 8
    vmem = pl.BlockSpec(memory_space=pltpu.VMEM)
    smem = pl.BlockSpec(memory_space=pltpu.SMEM)
    gathered, counts, own, mid = pl.pallas_call(
        functools.partial(gather_kernel, parts, slabs, depth),
        out_shape=(jax.ShapeDtypeStruct((total, LANES), jnp.float32),
                   jax.ShapeDtypeStruct((slabs, 8, LANES), jnp.int32),
                   jax.ShapeDtypeStruct((pipes, LANES), jnp.float32),
                   jax.ShapeDtypeStruct((1, 3, pipes, cells), jnp.float32)),
        in_specs=[vmem] * 5 + [smem],
        out_specs=(vmem,) * 4,
        scratch_shapes=[pltpu.VMEM((5, 3, LANES + 2 * HALO + 2 * PAD, LANES), jnp.float32),
                        pltpu.SemaphoreType.DMA((parts,)), pltpu.SemaphoreType.DMA((parts,)),
                        pltpu.SemaphoreType.DMA((slabs,)), pltpu.SemaphoreType.DMA((slabs,))],
        compiler_params=pltpu.CompilerParams(collective_id=0, has_side_effects=True),
        name="gather_ends",
    )(initial, wall_drag_factor, ground_exchange_rate, send_ends, recv_junction, slab_steps)
    return pl.pallas_call(
        functools.partial(solve_kernel, parts, slabs, depth),
        out_shape=jax.ShapeDtypeStruct((1, 3, pipes, cells), jnp.float32),
        in_specs=[vmem, vmem, vmem, smem],
        out_specs=vmem,
        scratch_shapes=[
            pltpu.VMEM((total, LANES), jnp.float32),
            pltpu.VMEM((slabs, 3, 2 * depth + 2 * PAD, total), jnp.float32),
            pltpu.VMEM((2, slabs, 3, 2 * depth + 2 * PAD, total), jnp.float32),
            pltpu.VMEM((slabs, 3, 2 * depth + 2 * PAD, total), jnp.float32),
            pltpu.VMEM((2 * total, 2 * total), jnp.bfloat16),
            pltpu.VMEM((1, 2 * total), jnp.float32),
            pltpu.VMEM((total, LANES), jnp.float32),
        ],
        name="solve",
    )(mid, own, gathered, counts)


def solution(mesh):
    return jax.shard_map(
        functools.partial(body, mesh.shape["net"], mesh.shape["tm"]),
        mesh=mesh,
        in_specs=(
            P(None, "net", None),
            P("net"),
            P("net"),
            P("net", None, None),
            P("net", None, None),
            P("tm"),
        ),
        out_specs=P("tm", None, "net", None),
        check_vma=False,
    )
```

```python
import functools

import jax
import jax.numpy as jnp
from jax import lax
from jax.experimental import pallas as pl
from jax.experimental.pallas import tpu as pltpu
from jax.sharding import PartitionSpec as P

STEPS_MAX = 8
STEPS_MIN = 4
STRIP = 16
LANES = 128
TABLE = 6 * STRIP
PAD = 8
HALO = 16
DRAG = TABLE + 8
GROUND = TABLE + 9
CODE_LEFT = TABLE + 10
CODE_RIGHT = TABLE + 11
MESH = pl.DeviceIdType.MESH


def roll(x, shift, axis):
    size = x.shape[axis]
    shift = shift % size
    return x if shift == 0 else pltpu.roll(x, shift, axis)


def column(row):
    pipes = row.shape[1]
    here = lax.broadcasted_iota(jnp.int32, (pipes, pipes), 0)
    there = lax.broadcasted_iota(jnp.int32, (pipes, pipes), 1)
    return jnp.sum(jnp.where(here == there, row, 0.0), axis=1, keepdims=True)


def sweep(source, targets, rows, chunk, h, drag, cool, live=None):
    for low in range(PAD, PAD + rows, chunk):
        here, prior, coming = (pl.ds(low + off, chunk) for off in (0, -1, 1))
        a, b, t = (source[f, here, :] for f in range(3))
        a_prior, t_prior = source[0, prior, :], source[2, prior, :]
        b_coming, t_coming = source[1, coming, :], source[2, coming, :]
        q = 0.5 * (a - b)
        if h is None:
            ahead, back = a_prior, b_coming
        else:
            ahead, back = a - h * (a - a_prior), b - h * (b - b_coming)
        p = 0.5 * (ahead + back)
        r = 0.5 * (ahead - back)
        slow = 1.0 + jnp.abs(q)
        dragged = 1.0 + drag * jnp.abs(r)
        inverse = 1.0 / (slow * dragged)
        flux = r * (slow * inverse)
        u = q * (dragged * inverse)
        gain = jnp.maximum(u, 0.0) * (t - t_prior) + jnp.minimum(u, 0.0) * (t_coming - t)
        if h is not None:
            gain = h * gain
        new = (p + flux, p - flux, (t - gain) * cool)
        if live is not None:
            new = tuple(jnp.where(live, x, y) for x, y in zip(new, (a, b, t)))
        for target in targets:
            for f in range(3):
                target[f, here, :] = new[f]


def gather_kernel(parts, slabs, depth, x_ref, drag_ref, ground_ref, send_ref, recv_ref, steps_ref,
                  all_ref, count_ref, deep_ref, mid_ref, fold_ref, send_sem, recv_sem, step_send_sem, step_recv_sem):
    me = lax.axis_index("net")
    slab = lax.axis_index("tm")
    pipes = x_ref.shape[1]
    cells = x_ref.shape[2]
    slots = send_ref.shape[2]
    barrier = pltpu.get_barrier_semaphore()
    for off in range(1, parts):
        pl.semaphore_signal(barrier, inc=1, device_id={"net": lax.rem(me + off, parts)},
                            device_id_type=MESH)
    for off in range(1, slabs):
        pl.semaphore_signal(barrier, inc=1, device_id={"tm": lax.rem(slab + off, slabs)},
                            device_id_type=MESH)

    lane = lax.broadcasted_iota(jnp.int32, (pipes, LANES), 1)
    block = jnp.zeros((pipes, LANES), jnp.float32)
    for f in range(3):
        base = 2 * STRIP * f
        left = roll(x_ref[f, :, 0:LANES], base, 1)
        right = roll(x_ref[f, :, cells - LANES:cells], base + 2 * STRIP - LANES, 1)
        block = jnp.where((lane >= base) & (lane < base + STRIP), left, block)
        block = jnp.where((lane >= base + STRIP) & (lane < base + 2 * STRIP), right, block)
    pipe = lax.broadcasted_iota(jnp.int32, (pipes, slots), 0)
    slot = lax.broadcasted_iota(jnp.int32, (pipes, slots), 1) + (me // pipes) * slots
    code_left = jnp.zeros((pipes, slots), jnp.int32)
    code_right = jnp.zeros((pipes, slots), jnp.int32)
    for d in range(parts):
        listed = send_ref[0, d:d + 1, :]
        code_left = jnp.where(listed == pipe, slot + 8 * d, code_left)
        code_right = jnp.where(listed == pipe + pipes, slot + 8 * d, code_right)
    code_left = jnp.sum(code_left.astype(jnp.float32), axis=1, keepdims=True)
    code_right = jnp.sum(code_right.astype(jnp.float32), axis=1, keepdims=True)
    for at, value in ((DRAG, column(drag_ref[...].reshape(1, pipes))),
                      (GROUND, column(ground_ref[...].reshape(1, pipes))),
                      (CODE_LEFT, code_left), (CODE_RIGHT, code_right)):
        block = jnp.where(lane == at, value, block)
    mine = pl.ds(pl.multiple_of(me * pipes, pipes), pipes)
    all_ref[mine, :] = block
    for g in range(-(-parts // pipes)):
        rows = min(pipes, parts - g * pipes)
        all_ref[pl.ds(pl.multiple_of(me * pipes, pipes), rows),
                TABLE + g * slots:TABLE + (g + 1) * slots] = (
            recv_ref[0, g * pipes:g * pipes + rows, :].astype(jnp.float32))
    count_ref[slab] = jnp.full((8, LANES), steps_ref[0], jnp.int32)

    segments = cells // LANES
    rows = LANES + 2 * HALO
    buffers = fold_ref.shape[0]
    fold_ref[:, :, 0:PAD, :] = jnp.zeros((buffers, 3, PAD, LANES), jnp.float32)
    fold_ref[:, :, PAD + rows:, :] = jnp.zeros((buffers, 3, PAD, LANES), jnp.float32)
    turned = [jnp.concatenate([x_ref[f, :, LANES * c:LANES * (c + 1)] for c in range(segments)],
                              0).T for f in range(3)]
    turned = (turned[0] + turned[1], turned[0] - turned[1], turned[2])
    for f in range(3):
        whole = jnp.concatenate([roll(turned[f][LANES - HALO:], pipes, 1), turned[f],
                                 roll(turned[f][:HALO], -pipes, 1)], 0)
        fold_ref[0, f, PAD:PAD + rows, :] = whole
        fold_ref[slabs + 1, f, PAD:PAD + rows, :] = whole

    own_pipe = (lane & (pipes - 1)) == lax.broadcasted_iota(jnp.int32, (pipes, LANES), 0)

    def in_lanes(ref):
        return jnp.sum(jnp.where(own_pipe, column(ref[...].reshape(1, pipes)), 0.0), axis=0,
                       keepdims=True)

    drag = in_lanes(drag_ref)
    ground = in_lanes(ground_ref)
    cool = 1.0 / (1.0 + ground)
    value, own_end, one, two = (fold_ref.at[slabs + 1 + k] for k in range(4))
    chunk = 40

    def guess(n, carry):
        sweep(fold_ref.at[n], [fold_ref.at[n + 1]], rows, chunk, None, drag, cool)
        return carry

    lax.fori_loop(0, slab + 1, guess, 0)

    pl.semaphore_wait(barrier, parts - 1 + slabs - 1)
    copies = []
    for off in range(1, slabs):
        copies.append(pltpu.make_async_remote_copy(
            src_ref=count_ref.at[slab], dst_ref=count_ref.at[slab],
            send_sem=step_send_sem.at[off], recv_sem=step_recv_sem.at[off],
            device_id={"tm": lax.rem(slab + off, slabs)}, device_id_type=MESH))
    for off in range(1, parts):
        copies.append(pltpu.make_async_remote_copy(
            src_ref=all_ref.at[mine], dst_ref=all_ref.at[mine],
            send_sem=send_sem.at[off], recv_sem=recv_sem.at[off],
            device_id={"net": lax.rem(me + off, parts)}, device_id_type=MESH))
    for copy in copies:
        copy.start()

    extra = depth - STRIP
    block = jnp.zeros((pipes, LANES), jnp.float32)
    for f in range(3):
        base = 2 * extra * f
        left = roll(x_ref[f, :, 0:LANES], base - STRIP, 1)
        right = roll(x_ref[f, :, cells - LANES:cells], base + extra - (LANES - depth), 1)
        block = jnp.where((lane >= base) & (lane < base + extra), left, block)
        block = jnp.where((lane >= base + extra) & (lane < base + 2 * extra), right, block)
    deep_ref[...] = block
    def fine(n, target):
        count = count_ref[n][0:1]
        h = 1.0 / count.astype(jnp.float32)
        drag_h = h * drag
        cool_h = 1.0 / (1.0 + h * ground)
        sweep(fold_ref.at[n], [one], rows, chunk, h, drag_h, cool_h)
        for source, sink in ((one, target), (target, one), (one, target)):
            sweep(source, [sink], rows, chunk, h, drag_h, cool_h)

        def pair(k, c):
            m = STEPS_MIN + 2 * k
            sweep(target, [one], rows, chunk, h, drag_h, cool_h, m < count)
            sweep(one, [target], rows, chunk, h, drag_h, cool_h, m + 1 < count)
            return c

        lax.fori_loop(0, (STEPS_MAX - STEPS_MIN) // 2, pair, 0)

    def correct(n, end):
        sweep(value, [one], rows, chunk, None, drag, cool)
        for low in range(PAD, PAD + rows, chunk):
            part = pl.ds(low, chunk)
            for f in range(3):
                value[f, part, :] = one[f, part, :] + (
                    end[f, part, :] - fold_ref[n + 1, f, part, :])

    fine(slab, own_end)
    for copy in copies[:slabs - 1]:
        copy.wait()

    def inner(n, carry):
        fine(n, two)
        correct(n, two)
        return carry

    lax.fori_loop(0, slab, inner, 0)
    correct(slab, own_end)
    middle = pl.ds(PAD + HALO, LANES)
    a, b, t = (value[f, middle, :] for f in range(3))
    for f, x in enumerate((0.5 * (a + b), 0.5 * (a - b), t)):
        back = x.T
        for c in range(segments):
            mid_ref[0, f, :, LANES * c:LANES * (c + 1)] = back[pipes * c:pipes * (c + 1)]
    for copy in copies[slabs - 1:]:
        copy.wait()


def solve_kernel(parts, slabs, depth, mid_ref, own_ref, all_ref, steps_ref, out_ref,
                 deep_ref, u_ref, s_ref, v_ref, adj_ref, inv_ref, back_ref):
    me = lax.axis_index("net")
    slab = lax.axis_index("tm")
    pipes = mid_ref.shape[2]
    cells = mid_ref.shape[3]
    total = parts * pipes
    junctions = pipes // 2
    reach = slabs + STEPS_MAX - 1
    extra = depth - STRIP
    f32, bf16, i32 = jnp.float32, jnp.bfloat16, jnp.int32
    mine = pl.ds(pl.multiple_of(me * pipes, pipes), pipes)

    deep_ref[...] = jnp.zeros_like(deep_ref)
    deep_ref[mine, :] = own_ref[...]
    deep = deep_ref[...].T
    shallow = all_ref[...].T
    rows = 2 * depth
    edge = PAD + rows
    ends = []
    for f in range(3):
        base = 2 * STRIP * f
        near = 2 * extra * f
        ends.append(jnp.concatenate([
            shallow[base:base + STRIP], deep[near:near + 2 * extra],
            shallow[base + STRIP:base + 2 * STRIP]], 0))
    for f, x in enumerate((ends[0] + ends[1], ends[0] - ends[1], ends[2])):
        s_ref[0, 0, f, PAD:edge, :] = x
    drag = shallow[DRAG:DRAG + 1]
    ground = shallow[GROUND:GROUND + 1]

    bits = pipes.bit_length() - 1
    source = lax.broadcasted_iota(i32, (total, total), 0)
    target = lax.broadcasted_iota(i32, (total, total), 1)
    spread = ((source & (pipes - 1)) == ((target >> bits) & (pipes - 1))).astype(f32).astype(bf16)
    table = shallow[TABLE:TABLE + 8]
    owner_of = lax.broadcasted_iota(i32, (8, total), 1) >> bits
    listed = jnp.concatenate([jnp.where(owner_of == d, table, 0.0) for d in range(parts)], 0)
    known = jnp.dot(listed.astype(bf16), spread, preferred_element_type=f32)
    place = lax.broadcasted_iota(i32, (8 * parts, total), 0)
    known = known + (junctions * (place >> 3)).astype(f32)
    names = []
    for at in (CODE_LEFT, CODE_RIGHT):
        hit = place.astype(f32) == shallow[at:at + 1]
        names.append(jnp.sum(jnp.where(hit, known, 0.0), axis=0, keepdims=True))
    name = jnp.concatenate(names, 1)
    number = lax.broadcasted_iota(i32, (parts * junctions, 2 * total), 0).astype(f32)
    member = (number == name).astype(f32).astype(bf16)
    meets = lax.dot_general(member, member, (((0,), (0,)), ((), ())), preferred_element_type=f32)
    adj_ref[...] = meets.astype(bf16)
    inv_ref[...] = 1.0 / jnp.sum(meets, axis=0, keepdims=True)

    def couple(states):
        count = len(states)
        height = -(-2 * count // 8) * 8
        at = lax.broadcasted_iota(i32, (height, 2 * total), 0)
        packed = jnp.zeros((height, 2 * total), f32)
        waves = []
        for n, state in enumerate(states):
            wave = jnp.concatenate(
                [state[1, PAD:PAD + 1, :], state[0, edge - 1:edge, :]], 1)
            waves.append(wave)
            warmth = jnp.concatenate(
                [state[2, PAD:PAD + 1, :], state[2, edge - 1:edge, :]], 1)
            packed = jnp.where(at == 2 * n, wave, packed)
            packed = jnp.where(at == 2 * n + 1, warmth, packed)
        high = packed.astype(bf16).astype(f32)
        rest = packed - high
        mid = rest.astype(bf16).astype(f32)
        split = jnp.concatenate([rest - mid, mid, high], 0).astype(bf16)
        sums = jnp.dot(split, adj_ref[...], preferred_element_type=f32)
        sums = sums[:height] + sums[height:2 * height] + sums[2 * height:]
        means = sums * inv_ref[...]
        for n, state in enumerate(states):
            z = 2.0 * means[2 * n:2 * n + 1] - waves[n]
            th = means[2 * n + 1:2 * n + 2]
            state[0, PAD - 1:PAD, :] = z[:, :total]
            state[1, edge:edge + 1, :] = z[:, total:]
            state[2, PAD - 1:PAD, :] = th[:, :total]
            state[2, edge:edge + 1, :] = th[:, total:]

    cool_one = 1.0 / (1.0 + ground)
    hs, drags, cools = [], [], []
    for n in range(slabs):
        h = 1.0 / (jnp.zeros((1, total), f32) + steps_ref[n, 0, 0].astype(f32))
        hs.append(h)
        drags.append(h * drag)
        cools.append(1.0 / (1.0 + h * ground))

    chunk = rows // 2
    last = STEPS_MAX + slabs - 2

    def fine(n, m):
        return s_ref.at[m % 2, n]

    def advance(n, m, also=()):
        live = None if m < STEPS_MIN else m < steps_ref[n, 0, 0]
        sweep(fine(n, m), [fine(n, m + 1), *also], rows, chunk, hs[n], drags[n], cools[n], live)

    for t in range(last + 1):
        active = [n for n in range(slabs) if 0 <= t - n < STEPS_MAX]
        states = [fine(n, t - n) for n in active]
        first = t - STEPS_MAX + 1
        if first >= 1:
            value = v_ref.at[first - 1]
            states.append(value)
        couple(states)
        if t < slabs:
            targets = [u_ref.at[t]] + ([fine(t + 1, 0)] if t + 1 < slabs else [])
            sweep(fine(t, 0), targets, rows, chunk, None, drag, cool_one)
        for n in active:
            advance(n, t - n, [v_ref.at[0]] if n == 0 and t == STEPS_MAX - 1 else [])
        if first >= 1:
            sweep(value, [v_ref.at[first]], rows, chunk, None, drag, cool_one)
            for f in range(3):
                v_ref[first, f, PAD:edge, :] = v_ref[first, f, PAD:edge, :] + (
                    s_ref[0, first, f, PAD:edge, :] - u_ref[first, f, PAD:edge, :])
    pieces = []
    for span in (pl.ds(PAD, STRIP), pl.ds(edge - STRIP, STRIP)):
        a, b, t = (v_ref[slab, f, span, :] for f in range(3))
        pieces.append((0.5 * (a + b), 0.5 * (a - b), t))
    pieces = [side[f] for f in range(3) for side in pieces]
    pieces.append(jnp.zeros((LANES - TABLE, total), f32))
    back_ref[...] = jnp.concatenate(pieces, 0).T
    ends = back_ref[mine, :]
    lane = lax.broadcasted_iota(i32, (pipes, LANES), 1)
    for f in range(3):
        base = 2 * STRIP * f
        out_ref[0, f, :, LANES:cells - LANES] = mid_ref[0, f, :, LANES:cells - LANES]
        out_ref[0, f, :, 0:LANES] = jnp.where(
            lane < reach, roll(ends, -base, 1), mid_ref[0, f, :, 0:LANES])
        out_ref[0, f, :, cells - LANES:cells] = jnp.where(
            lane >= LANES - reach, roll(ends, LANES - 2 * STRIP - base, 1),
            mid_ref[0, f, :, cells - LANES:cells])


def body(parts, slabs, initial, wall_drag_factor, ground_exchange_rate, send_ends, recv_junction,
         slab_steps):
    pipes, cells = initial.shape[1:]
    total = parts * pipes
    depth = -(-2 * (slabs + STEPS_MAX - 1) // 8) * 8
    vmem = pl.BlockSpec(memory_space=pltpu.VMEM)
    smem = pl.BlockSpec(memory_space=pltpu.SMEM)
    gathered, counts, own, mid = pl.pallas_call(
        functools.partial(gather_kernel, parts, slabs, depth),
        out_shape=(jax.ShapeDtypeStruct((total, LANES), jnp.float32),
                   jax.ShapeDtypeStruct((slabs, 8, LANES), jnp.int32),
                   jax.ShapeDtypeStruct((pipes, LANES), jnp.float32),
                   jax.ShapeDtypeStruct((1, 3, pipes, cells), jnp.float32)),
        in_specs=[vmem] * 5 + [smem],
        out_specs=(vmem,) * 4,
        scratch_shapes=[pltpu.VMEM((slabs + 5, 3, LANES + 2 * HALO + 2 * PAD, LANES), jnp.float32),
                        pltpu.SemaphoreType.DMA((parts,)), pltpu.SemaphoreType.DMA((parts,)),
                        pltpu.SemaphoreType.DMA((slabs,)), pltpu.SemaphoreType.DMA((slabs,))],
        compiler_params=pltpu.CompilerParams(collective_id=0, has_side_effects=True),
        name="gather_ends",
    )(initial, wall_drag_factor, ground_exchange_rate, send_ends, recv_junction, slab_steps)
    return pl.pallas_call(
        functools.partial(solve_kernel, parts, slabs, depth),
        out_shape=jax.ShapeDtypeStruct((1, 3, pipes, cells), jnp.float32),
        in_specs=[vmem, vmem, vmem, smem],
        out_specs=vmem,
        scratch_shapes=[
            pltpu.VMEM((total, LANES), jnp.float32),
            pltpu.VMEM((slabs, 3, 2 * depth + 2 * PAD, total), jnp.float32),
            pltpu.VMEM((2, slabs, 3, 2 * depth + 2 * PAD, total), jnp.float32),
            pltpu.VMEM((slabs, 3, 2 * depth + 2 * PAD, total), jnp.float32),
            pltpu.VMEM((2 * total, 2 * total), jnp.bfloat16),
            pltpu.VMEM((1, 2 * total), jnp.float32),
            pltpu.VMEM((total, LANES), jnp.float32),
        ],
        name="solve",
    )(mid, own, gathered, counts)


def solution(mesh):
    return jax.shard_map(
        functools.partial(body, mesh.shape["net"], mesh.shape["tm"]),
        mesh=mesh,
        in_specs=(
            P(None, "net", None),
            P("net"),
            P("net"),
            P("net", None, None),
            P("net", None, None),
            P("tm"),
        ),
        out_specs=P("tm", None, "net", None),
        check_vma=False,
    )
```

```python
import functools

import jax
import jax.numpy as jnp
from jax import lax
from jax.experimental import pallas as pl
from jax.experimental.pallas import tpu as pltpu
from jax.sharding import PartitionSpec as P

STEPS_MAX = 8
STEPS_MIN = 4
STRIP = 16
LANES = 128
TABLE = 6 * STRIP
PAD = 8
HALO = 16
DRAG = TABLE + 8
GROUND = TABLE + 9
CODE_LEFT = TABLE + 10
CODE_RIGHT = TABLE + 11
MESH = pl.DeviceIdType.MESH


def roll(x, shift, axis):
    size = x.shape[axis]
    shift = shift % size
    return x if shift == 0 else pltpu.roll(x, shift, axis)


def column(row):
    pipes = row.shape[1]
    here = lax.broadcasted_iota(jnp.int32, (pipes, pipes), 0)
    there = lax.broadcasted_iota(jnp.int32, (pipes, pipes), 1)
    return jnp.sum(jnp.where(here == there, row, 0.0), axis=1, keepdims=True)


def sweep(source, targets, rows, chunk, h, drag, cool, live=None):
    for low in range(PAD, PAD + rows, chunk):
        here, prior, coming = (pl.ds(low + off, chunk) for off in (0, -1, 1))
        a, b, t = (source[f, here, :] for f in range(3))
        a_prior, t_prior = source[0, prior, :], source[2, prior, :]
        b_coming, t_coming = source[1, coming, :], source[2, coming, :]
        q = 0.5 * (a - b)
        if h is None:
            ahead, back = a_prior, b_coming
        else:
            ahead, back = a - h * (a - a_prior), b - h * (b - b_coming)
        p = 0.5 * (ahead + back)
        r = 0.5 * (ahead - back)
        slow = 1.0 + jnp.abs(q)
        dragged = 1.0 + drag * jnp.abs(r)
        inverse = 1.0 / (slow * dragged)
        flux = r * (slow * inverse)
        u = q * (dragged * inverse)
        gain = jnp.maximum(u, 0.0) * (t - t_prior) + jnp.minimum(u, 0.0) * (t_coming - t)
        if h is not None:
            gain = h * gain
        new = (p + flux, p - flux, (t - gain) * cool)
        if live is not None:
            new = tuple(jnp.where(live, x, y) for x, y in zip(new, (a, b, t)))
        for target in targets:
            for f in range(3):
                target[f, here, :] = new[f]


def gather_kernel(parts, slabs, depth, x_ref, drag_ref, ground_ref, send_ref, recv_ref, steps_ref,
                  all_ref, count_ref, deep_ref, mid_ref, fold_ref, send_sem, recv_sem, step_send_sem, step_recv_sem):
    me = lax.axis_index("net")
    slab = lax.axis_index("tm")
    pipes = x_ref.shape[1]
    cells = x_ref.shape[2]
    slots = send_ref.shape[2]
    barrier = pltpu.get_barrier_semaphore()
    for off in range(1, parts):
        pl.semaphore_signal(barrier, inc=1, device_id={"net": lax.rem(me + off, parts)},
                            device_id_type=MESH)
    for off in range(1, slabs):
        pl.semaphore_signal(barrier, inc=1, device_id={"tm": lax.rem(slab + off, slabs)},
                            device_id_type=MESH)

    lane = lax.broadcasted_iota(jnp.int32, (pipes, LANES), 1)
    block = jnp.zeros((pipes, LANES), jnp.float32)
    for f in range(3):
        base = 2 * STRIP * f
        left = roll(x_ref[f, :, 0:LANES], base, 1)
        right = roll(x_ref[f, :, cells - LANES:cells], base + 2 * STRIP - LANES, 1)
        block = jnp.where((lane >= base) & (lane < base + STRIP), left, block)
        block = jnp.where((lane >= base + STRIP) & (lane < base + 2 * STRIP), right, block)
    pipe = lax.broadcasted_iota(jnp.int32, (pipes, slots), 0)
    slot = lax.broadcasted_iota(jnp.int32, (pipes, slots), 1) + (me // pipes) * slots
    code_left = jnp.zeros((pipes, slots), jnp.int32)
    code_right = jnp.zeros((pipes, slots), jnp.int32)
    for d in range(parts):
        listed = send_ref[0, d:d + 1, :]
        code_left = jnp.where(listed == pipe, slot + 8 * d, code_left)
        code_right = jnp.where(listed == pipe + pipes, slot + 8 * d, code_right)
    code_left = jnp.sum(code_left.astype(jnp.float32), axis=1, keepdims=True)
    code_right = jnp.sum(code_right.astype(jnp.float32), axis=1, keepdims=True)
    for at, value in ((DRAG, column(drag_ref[...].reshape(1, pipes))),
                      (GROUND, column(ground_ref[...].reshape(1, pipes))),
                      (CODE_LEFT, code_left), (CODE_RIGHT, code_right)):
        block = jnp.where(lane == at, value, block)
    mine = pl.ds(pl.multiple_of(me * pipes, pipes), pipes)
    all_ref[mine, :] = block
    for g in range(-(-parts // pipes)):
        rows = min(pipes, parts - g * pipes)
        all_ref[pl.ds(pl.multiple_of(me * pipes, pipes), rows),
                TABLE + g * slots:TABLE + (g + 1) * slots] = (
            recv_ref[0, g * pipes:g * pipes + rows, :].astype(jnp.float32))
    count_ref[slab] = jnp.broadcast_to(steps_ref[...].reshape(1, 1), (8, LANES))

    segments = cells // LANES
    rows = LANES + 2 * HALO
    buffers = fold_ref.shape[0]
    fold_ref[:, :, 0:PAD, :] = jnp.zeros((buffers, 3, PAD, LANES), jnp.float32)
    fold_ref[:, :, PAD + rows:, :] = jnp.zeros((buffers, 3, PAD, LANES), jnp.float32)
    turned = [jnp.concatenate([x_ref[f, :, LANES * c:LANES * (c + 1)] for c in range(segments)],
                              0).T for f in range(3)]
    turned = (turned[0] + turned[1], turned[0] - turned[1], turned[2])
    for f in range(3):
        whole = jnp.concatenate([roll(turned[f][LANES - HALO:], pipes, 1), turned[f],
                                 roll(turned[f][:HALO], -pipes, 1)], 0)
        fold_ref[0, f, PAD:PAD + rows, :] = whole
        fold_ref[slabs + 1, f, PAD:PAD + rows, :] = whole

    own_pipe = (lane & (pipes - 1)) == lax.broadcasted_iota(jnp.int32, (pipes, LANES), 0)

    def in_lanes(ref):
        return jnp.sum(jnp.where(own_pipe, column(ref[...].reshape(1, pipes)), 0.0), axis=0,
                       keepdims=True)

    drag = in_lanes(drag_ref)
    ground = in_lanes(ground_ref)
    cool = 1.0 / (1.0 + ground)
    value, own_end, one, two = (fold_ref.at[slabs + 1 + k] for k in range(4))
    chunk = 40

    def guess(n, carry):
        sweep(fold_ref.at[n], [fold_ref.at[n + 1]], rows, chunk, None, drag, cool)
        return carry

    lax.fori_loop(0, slab + 1, guess, 0)

    pl.semaphore_wait(barrier, parts - 1 + slabs - 1)
    copies = []
    for off in range(1, slabs):
        copies.append(pltpu.make_async_remote_copy(
            src_ref=count_ref.at[slab], dst_ref=count_ref.at[slab],
            send_sem=step_send_sem.at[off], recv_sem=step_recv_sem.at[off],
            device_id={"tm": lax.rem(slab + off, slabs)}, device_id_type=MESH))
    for off in range(1, parts):
        copies.append(pltpu.make_async_remote_copy(
            src_ref=all_ref.at[mine], dst_ref=all_ref.at[mine],
            send_sem=send_sem.at[off], recv_sem=recv_sem.at[off],
            device_id={"net": lax.rem(me + off, parts)}, device_id_type=MESH))
    for copy in copies:
        copy.start()

    extra = depth - STRIP
    block = jnp.zeros((pipes, LANES), jnp.float32)
    for f in range(3):
        base = 2 * extra * f
        left = roll(x_ref[f, :, 0:LANES], base - STRIP, 1)
        right = roll(x_ref[f, :, cells - LANES:cells], base + extra - (LANES - depth), 1)
        block = jnp.where((lane >= base) & (lane < base + extra), left, block)
        block = jnp.where((lane >= base + extra) & (lane < base + 2 * extra), right, block)
    deep_ref[...] = block

    def fine(n, target):
        count = count_ref[n][0:1]
        h = 1.0 / count.astype(jnp.float32)
        drag_h = h * drag
        cool_h = 1.0 / (1.0 + h * ground)
        sweep(fold_ref.at[n], [one], rows, chunk, h, drag_h, cool_h)
        for source, sink in ((one, target), (target, one), (one, target)):
            sweep(source, [sink], rows, chunk, h, drag_h, cool_h)

        def pair(k, c):
            m = STEPS_MIN + 2 * k
            sweep(target, [one], rows, chunk, h, drag_h, cool_h, m < count)
            sweep(one, [target], rows, chunk, h, drag_h, cool_h, m + 1 < count)
            return c

        lax.fori_loop(0, (STEPS_MAX - STEPS_MIN) // 2, pair, 0)

    def correct(n, end):
        sweep(value, [one], rows, chunk, None, drag, cool)
        for low in range(PAD, PAD + rows, chunk):
            part = pl.ds(low, chunk)
            for f in range(3):
                value[f, part, :] = one[f, part, :] + (
                    end[f, part, :] - fold_ref[n + 1, f, part, :])

    fine(slab, own_end)
    for copy in copies[:slabs - 1]:
        copy.wait()

    def inner(n, carry):
        fine(n, two)
        correct(n, two)
        return carry

    lax.fori_loop(0, slab, inner, 0)
    correct(slab, own_end)
    middle = pl.ds(PAD + HALO, LANES)
    a, b, t = (value[f, middle, :] for f in range(3))
    for f, x in enumerate((0.5 * (a + b), 0.5 * (a - b), t)):
        back = x.T
        for c in range(segments):
            mid_ref[0, f, :, LANES * c:LANES * (c + 1)] = back[pipes * c:pipes * (c + 1)]
    for copy in copies[slabs - 1:]:
        copy.wait()


def solve_kernel(parts, slabs, depth, mid_ref, own_ref, all_ref, steps_ref, out_ref,
                 deep_ref, u_ref, s_ref, v_ref, adj_ref, inv_ref, back_ref):
    me = lax.axis_index("net")
    slab = lax.axis_index("tm")
    pipes = mid_ref.shape[2]
    cells = mid_ref.shape[3]
    total = parts * pipes
    junctions = pipes // 2
    reach = slabs + STEPS_MAX - 1
    extra = depth - STRIP
    f32, bf16, i32 = jnp.float32, jnp.bfloat16, jnp.int32
    mine = pl.ds(pl.multiple_of(me * pipes, pipes), pipes)

    deep_ref[...] = jnp.zeros_like(deep_ref)
    deep_ref[mine, :] = own_ref[...]
    deep = deep_ref[...].T
    shallow = all_ref[...].T
    rows = 2 * depth
    edge = PAD + rows
    ends = []
    for f in range(3):
        base = 2 * STRIP * f
        near = 2 * extra * f
        ends.append(jnp.concatenate([
            shallow[base:base + STRIP], deep[near:near + 2 * extra],
            shallow[base + STRIP:base + 2 * STRIP]], 0))
    for f, x in enumerate((ends[0] + ends[1], ends[0] - ends[1], ends[2])):
        s_ref[0, 0, f, PAD:edge, :] = x
    drag = shallow[DRAG:DRAG + 1]
    ground = shallow[GROUND:GROUND + 1]

    bits = pipes.bit_length() - 1
    source = lax.broadcasted_iota(i32, (total, total), 0)
    target = lax.broadcasted_iota(i32, (total, total), 1)
    spread = ((source & (pipes - 1)) == ((target >> bits) & (pipes - 1))).astype(f32).astype(bf16)
    table = shallow[TABLE:TABLE + 8]
    owner_of = lax.broadcasted_iota(i32, (8, total), 1) >> bits
    listed = jnp.concatenate([jnp.where(owner_of == d, table, 0.0) for d in range(parts)], 0)
    known = jnp.dot(listed.astype(bf16), spread, preferred_element_type=f32)
    place = lax.broadcasted_iota(i32, (8 * parts, total), 0)
    known = known + (junctions * (place >> 3)).astype(f32)
    names = []
    for at in (CODE_LEFT, CODE_RIGHT):
        hit = place.astype(f32) == shallow[at:at + 1]
        names.append(jnp.sum(jnp.where(hit, known, 0.0), axis=0, keepdims=True))
    name = jnp.concatenate(names, 1)
    number = lax.broadcasted_iota(i32, (parts * junctions, 2 * total), 0).astype(f32)
    member = (number == name).astype(f32).astype(bf16)
    meets = lax.dot_general(member, member, (((0,), (0,)), ((), ())), preferred_element_type=f32)
    adj_ref[...] = meets.astype(bf16)
    inv_ref[...] = 1.0 / jnp.sum(meets, axis=0, keepdims=True)

    def couple(states):
        count = len(states)
        height = -(-2 * count // 8) * 8
        at = lax.broadcasted_iota(i32, (height, 2 * total), 0)
        packed = jnp.zeros((height, 2 * total), f32)
        waves = []
        for n, state in enumerate(states):
            wave = jnp.concatenate(
                [state[1, PAD:PAD + 1, :], state[0, edge - 1:edge, :]], 1)
            waves.append(wave)
            warmth = jnp.concatenate(
                [state[2, PAD:PAD + 1, :], state[2, edge - 1:edge, :]], 1)
            packed = jnp.where(at == 2 * n, wave, packed)
            packed = jnp.where(at == 2 * n + 1, warmth, packed)
        high = packed.astype(bf16).astype(f32)
        rest = packed - high
        mid = rest.astype(bf16).astype(f32)
        split = jnp.concatenate([rest - mid, mid, high], 0).astype(bf16)
        sums = jnp.dot(split, adj_ref[...], preferred_element_type=f32)
        sums = sums[:height] + sums[height:2 * height] + sums[2 * height:]
        means = sums * inv_ref[...]
        for n, state in enumerate(states):
            z = 2.0 * means[2 * n:2 * n + 1] - waves[n]
            th = means[2 * n + 1:2 * n + 2]
            state[0, PAD - 1:PAD, :] = z[:, :total]
            state[1, edge:edge + 1, :] = z[:, total:]
            state[2, PAD - 1:PAD, :] = th[:, :total]
            state[2, edge:edge + 1, :] = th[:, total:]

    cool_one = 1.0 / (1.0 + ground)
    counts, hs, drags, cools = [], [], [], []
    for n in range(slabs):
        count = jnp.concatenate([steps_ref[n][0:1]] * (total // LANES), 1)
        h = 1.0 / count.astype(f32)
        counts.append(count)
        hs.append(h)
        drags.append(h * drag)
        cools.append(1.0 / (1.0 + h * ground))

    chunk = rows // 2
    last = STEPS_MAX + slabs - 2

    def fine(n, m):
        return s_ref.at[m % 2, n]

    def advance(n, m, also=()):
        live = None if m < STEPS_MIN else m < counts[n]
        sweep(fine(n, m), [fine(n, m + 1), *also], rows, chunk, hs[n], drags[n], cools[n], live)

    for t in range(last + 1):
        active = [n for n in range(slabs) if 0 <= t - n < STEPS_MAX]
        states = [fine(n, t - n) for n in active]
        first = t - STEPS_MAX + 1
        if first >= 1:
            value = v_ref.at[first - 1]
            states.append(value)
        couple(states)
        if t < slabs:
            targets = [u_ref.at[t]] + ([fine(t + 1, 0)] if t + 1 < slabs else [])
            sweep(fine(t, 0), targets, rows, chunk, None, drag, cool_one)
        for n in active:
            advance(n, t - n, [v_ref.at[0]] if n == 0 and t == STEPS_MAX - 1 else [])
        if first >= 1:
            sweep(value, [v_ref.at[first]], rows, chunk, None, drag, cool_one)
            for f in range(3):
                v_ref[first, f, PAD:edge, :] = v_ref[first, f, PAD:edge, :] + (
                    s_ref[0, first, f, PAD:edge, :] - u_ref[first, f, PAD:edge, :])
    pieces = []
    for span in (pl.ds(PAD, STRIP), pl.ds(edge - STRIP, STRIP)):
        a, b, t = (v_ref[slab, f, span, :] for f in range(3))
        pieces.append((0.5 * (a + b), 0.5 * (a - b), t))
    pieces = [side[f] for f in range(3) for side in pieces]
    pieces.append(jnp.zeros((LANES - TABLE, total), f32))
    back_ref[...] = jnp.concatenate(pieces, 0).T
    ends = back_ref[mine, :]
    lane = lax.broadcasted_iota(i32, (pipes, LANES), 1)
    for f in range(3):
        base = 2 * STRIP * f
        out_ref[0, f, :, LANES:cells - LANES] = mid_ref[0, f, :, LANES:cells - LANES]
        out_ref[0, f, :, 0:LANES] = jnp.where(
            lane < reach, roll(ends, -base, 1), mid_ref[0, f, :, 0:LANES])
        out_ref[0, f, :, cells - LANES:cells] = jnp.where(
            lane >= LANES - reach, roll(ends, LANES - 2 * STRIP - base, 1),
            mid_ref[0, f, :, cells - LANES:cells])


def body(parts, slabs, initial, wall_drag_factor, ground_exchange_rate, send_ends, recv_junction,
         slab_steps):
    pipes, cells = initial.shape[1:]
    total = parts * pipes
    depth = -(-2 * (slabs + STEPS_MAX - 1) // 8) * 8
    vmem = pl.BlockSpec(memory_space=pltpu.VMEM)
    gathered, counts, own, mid = pl.pallas_call(
        functools.partial(gather_kernel, parts, slabs, depth),
        out_shape=(jax.ShapeDtypeStruct((total, LANES), jnp.float32),
                   jax.ShapeDtypeStruct((slabs, 8, LANES), jnp.int32),
                   jax.ShapeDtypeStruct((pipes, LANES), jnp.float32),
                   jax.ShapeDtypeStruct((1, 3, pipes, cells), jnp.float32)),
        in_specs=[vmem] * 6,
        out_specs=(vmem,) * 4,
        scratch_shapes=[pltpu.VMEM((slabs + 5, 3, LANES + 2 * HALO + 2 * PAD, LANES), jnp.float32),
                        pltpu.SemaphoreType.DMA((parts,)), pltpu.SemaphoreType.DMA((parts,)),
                        pltpu.SemaphoreType.DMA((slabs,)), pltpu.SemaphoreType.DMA((slabs,))],
        compiler_params=pltpu.CompilerParams(collective_id=0, has_side_effects=True),
        name="gather_ends",
    )(initial, wall_drag_factor, ground_exchange_rate, send_ends, recv_junction, slab_steps)
    return pl.pallas_call(
        functools.partial(solve_kernel, parts, slabs, depth),
        out_shape=jax.ShapeDtypeStruct((1, 3, pipes, cells), jnp.float32),
        in_specs=[vmem] * 4,
        out_specs=vmem,
        scratch_shapes=[
            pltpu.VMEM((total, LANES), jnp.float32),
            pltpu.VMEM((slabs, 3, 2 * depth + 2 * PAD, total), jnp.float32),
            pltpu.VMEM((2, slabs, 3, 2 * depth + 2 * PAD, total), jnp.float32),
            pltpu.VMEM((slabs, 3, 2 * depth + 2 * PAD, total), jnp.float32),
            pltpu.VMEM((2 * total, 2 * total), jnp.bfloat16),
            pltpu.VMEM((1, 2 * total), jnp.float32),
            pltpu.VMEM((total, LANES), jnp.float32),
        ],
        name="solve",
    )(mid, own, gathered, counts)


def solution(mesh):
    return jax.shard_map(
        functools.partial(body, mesh.shape["net"], mesh.shape["tm"]),
        mesh=mesh,
        in_specs=(
            P(None, "net", None),
            P("net"),
            P("net"),
            P("net", None, None),
            P("net", None, None),
            P("tm"),
        ),
        out_specs=P("tm", None, "net", None),
        check_vma=False,
    )
```
